32 devices in a mesh: groups: 2 (over y), row: 8 (over z, x), col: 2 (over core).
Axes of the slice: x: 2, y: 2, z: 4, core: 2. Of those that a mesh axis runs over, the one named last changes fastest.
Arguments:
- embeddings: bfloat16 [128, 16, 1280], P(('groups', 'row'), 'col'), parts along dimension 0, may hold values from -6 to 52
- pos_embed: bfloat16 [256, 1280], replicated, may hold values from -3 to 3
- ln_gain: float32 [1280], replicated, may hold values from 0.6 to 9
- ln_bias: float32 [1280], replicated, may hold values from -1.5 to 1.5
- w_qkv: bfloat16 [1280, 1920], P(('row', 'col')), may hold values from -0.25155765 to 0.25155765
- b_qkv: float32 [1920], replicated, may hold values from -1.5 to 1.5
- w_out: bfloat16 [1280, 640], P(('row', 'col')), may hold values from -0.25 to 0.25
- b_out: float32 [1280], replicated, may hold values from -1.5 to 1.5
- valid: int32 [16, 2, 256], P(('groups', 'row'), 'col'), parts along dimension 0, may hold values from 0 to 196
Outputs:
- merged: bfloat16 [128, 16, 1280], P(('groups', 'row'), 'col'), parts along dimension 0
The draws below stay inside these ranges and needn't reach their ends.
There are 2 independent parts, one for each index of `groups`. The reference program is written for one: setup_inputs(seed, part) draws one part's arguments, and reference() takes and returns one part's arrays. A program takes and returns all parts, laid end to end along the dimension named above; an argument that names none is the same for every part. Nothing has to cross between parts.
All inputs are finite; a program needn't handle non-finite values.
Results may differ from the reference program's by a relative error of at most 0.0098.
Values may be sent and summed in bfloat16 or wider, within the bound.
A program may use at most 64 MiB of HBM per device.

```python
import jax
import jax.numpy as jnp
from jax import lax

D = 1280
HEADS = 8
HEAD_DIM = 80
TILE = 8
HD = 640
QKV = 1920
WIN = 16
RIM = 4
TOK = 256
TROWS = 8
NPR = 64
NPC = 16
N_COL = 2


def draw_embeddings(key, part):
    first = jax.random.fold_in(key, 0)
    values = jnp.clip(jax.random.normal(first, (NPR, NPC, D), jnp.float32), -6.0, 6.0)
    return values.astype(jnp.bfloat16)


def draw_ln_gain(key, part):
    first = jax.random.fold_in(key, 0)
    base = jax.random.uniform(first, (D,), jnp.float32, 0.6, 1.4)
    return base


def draw_w_qkv(key, part):
    full = jnp.clip(jax.random.normal(key, (D, QKV), jnp.float32), -6.0, 6.0) * D ** (-0.5)
    return full.astype(jnp.bfloat16)


def plant(entries, stream_key, low, high):
    spot = [jax.random.randint(jax.random.fold_in(stream_key, axis), (), 0, length) for axis, length in enumerate(entries.shape)]
    widest = entries.shape.index(max(entries.shape))
    beside = spot[:widest] + [(spot[widest] + 1) % entries.shape[widest]] + spot[widest + 1:]
    return entries.at[tuple(spot)].set(low).at[tuple(beside)].set(high)


def level_of(stream_key, shape, cuts, least, top_value):
    loudness, own = 1.0, jax.random.fold_in(stream_key, 6)
    for axis_at, parts in cuts:
        heights = jnp.exp(jax.random.uniform(jax.random.fold_in(own, axis_at), (parts,), jnp.float32, least / len(cuts), top_value / len(cuts)))
        loudness = loudness * jnp.repeat(heights, shape[axis_at] // parts).reshape([-1 if axis == axis_at else 1 for axis in range(len(shape))])
    return loudness


def bell_draw(key, extent, spread, limit, cuts=(), held_as=jnp.bfloat16):
    entries = spread * jax.random.normal(key, extent, jnp.float32)
    if cuts:
        entries = entries * level_of(key, extent, cuts, -0.22, 0.18)
    return jnp.clip(entries, -limit, limit).astype(held_as)


def setup_inputs(seed: int = 0, part: int = 0) -> dict:
    key_list = jax.random.split(jax.random.key(seed), 10)
    own_keys = jax.random.split(jax.random.fold_in(key_list[9], part), 10)
    embeddings = draw_embeddings(jax.random.fold_in(jax.random.fold_in(key_list[9], part), 71), part)
    pos_embed = bell_draw(key_list[1], (TOK, D), 0.5, 3.0)
    ln_gain = draw_ln_gain(jax.random.fold_in(key_list[9], 71), part)
    ln_bias = bell_draw(key_list[3], (D,), 0.3, 1.5, (), jnp.float32)
    w_qkv = draw_w_qkv(jax.random.fold_in(key_list[9], 71), part)
    b_qkv = bell_draw(key_list[5], (QKV,), 0.3, 1.5, (), jnp.float32)
    w_out = bell_draw(key_list[6], (D, HD), HD ** -0.5, 0.25, ((0, 16),))
    b_out = bell_draw(key_list[7], (D,), 0.3, 1.5, (), jnp.float32)
    valid = plant(jax.random.randint(own_keys[8], (TROWS, N_COL, TOK), 0, 197), jax.random.fold_in(own_keys[8], 1), 0, 196).astype(jnp.int32)
    return dict(embeddings=embeddings, pos_embed=pos_embed, ln_gain=ln_gain, ln_bias=ln_bias, w_qkv=w_qkv, b_qkv=b_qkv, w_out=w_out, b_out=b_out, valid=valid)


EPSILON = 1e-06
SPREAD = 4.0
FLOOR = 0.25

def layer_norm(inputs, ln_gain, ln_bias):
    centred = inputs - lax.optimization_barrier(jnp.mean(inputs, axis=-1, keepdims=True))
    variance = lax.optimization_barrier(jnp.mean(centred * centred, axis=-1, keepdims=True))
    return centred * lax.rsqrt(variance + EPSILON) * ln_gain + ln_bias

def gauss_table(win):
    offsets = jnp.arange(win, dtype=jnp.float32) - (win - 1) / 2.0
    squared = offsets[:, None] * offsets[:, None] + offsets[None, :] * offsets[None, :]
    return jnp.exp(-squared / (2.0 * SPREAD * SPREAD))

def attend(projected):
    rows_count = projected.shape[0]
    queries = projected[:, :HD].reshape(rows_count, HEADS, HEAD_DIM).astype(jnp.float32)
    keys = projected[:, HD:2 * HD].reshape(rows_count, HEADS, HEAD_DIM).astype(jnp.float32)
    values = projected[:, 2 * HD:].reshape(rows_count, HEADS, HEAD_DIM).astype(jnp.float32)
    scores = jnp.einsum('qhd,khd->hqk', queries, keys) * HEAD_DIM ** (-0.5)
    highest = lax.optimization_barrier(jnp.max(scores, axis=-1, keepdims=True))
    expon = jnp.exp(scores - highest)
    probs = (expon / lax.optimization_barrier(jnp.sum(expon, axis=-1, keepdims=True))).astype(jnp.bfloat16)
    mixed = jnp.einsum('hqk,khd->qhd', probs.astype(jnp.float32), values)
    return mixed.astype(jnp.bfloat16).reshape(rows_count, HD)

def reference(embeddings, pos_embed, ln_gain, ln_bias, w_qkv, b_qkv, w_out, b_out, valid):
    padded = jnp.pad(embeddings, ((RIM, RIM), (RIM, RIM), (0, 0)))
    gauss = gauss_table(WIN).reshape(TOK)
    zero_index = jnp.zeros((), jnp.int32)

    def one_window(carry, index):
        numer, denom = carry
        row_at = (index // N_COL).astype(jnp.int32)
        col_at = (index % N_COL).astype(jnp.int32)
        patch = lax.dynamic_slice(padded, (row_at * TILE, col_at * TILE, zero_index), (WIN, WIN, D))
        inputs = patch.reshape(TOK, D).astype(jnp.float32) + pos_embed.astype(jnp.float32)
        normed = layer_norm(inputs, ln_gain, ln_bias).astype(jnp.bfloat16)
        projected = (jnp.dot(normed, w_qkv, preferred_element_type=jnp.float32) + b_qkv).astype(jnp.bfloat16)
        attended = attend(projected)
        hidden = inputs + jnp.dot(attended, w_out.T, preferred_element_type=jnp.float32) + b_out
        counts = lax.dynamic_slice(valid, (row_at, col_at, zero_index), (1, 1, TOK)).reshape(TOK)
        weight = gauss * counts.astype(jnp.float32) / 196.0
        add_numer = (weight[:, None] * hidden).reshape(WIN, WIN, D)
        add_denom = weight.reshape(WIN, WIN)
        start = (row_at * TILE, col_at * TILE, zero_index)
        numer = lax.dynamic_update_slice(numer, lax.dynamic_slice(numer, start, (WIN, WIN, D)) + add_numer, start)
        dstart = (row_at * TILE, col_at * TILE)
        denom = lax.dynamic_update_slice(denom, lax.dynamic_slice(denom, dstart, (WIN, WIN)) + add_denom, dstart)
        return ((numer, denom), None)
    init = (jnp.zeros((NPR + 2 * RIM, NPC + 2 * RIM, D), jnp.float32), jnp.zeros((NPR + 2 * RIM, NPC + 2 * RIM), jnp.float32))
    (numer, denom), _ = lax.scan(one_window, init, jnp.arange(TROWS * N_COL, dtype=jnp.int32))
    numer = numer[RIM:RIM + NPR, RIM:RIM + NPC]
    denom = denom[RIM:RIM + NPR, RIM:RIM + NPC]
    return (numer / jnp.maximum(denom, FLOOR)[:, :, None]).astype(jnp.bfloat16)
```

```python
import functools

import jax
import jax.numpy as jnp
from jax import lax
from jax.experimental import pallas as pl
from jax.experimental.pallas import tpu as pltpu
from jax.sharding import PartitionSpec as P

HEADS = 8
EPSILON = 1e-06
SPREAD = 4.0
FLOOR = 0.25
LANES = 128
MESH = pl.DeviceIdType.MESH


def kernel(
    rows,
    emb_ref, pos_ref, gain_ref, bias_ref, wq_ref, bq_ref, wo_ref, bo_ref, valid_ref,
    out_ref,
    eb, vb, wq_all, wo_all, nrm, proj, posr, base, wcol, att, rim_out, rim_in,
    top_out, top_in, bot_out, bot_in, send_sems, recv_sems, local_sems,
):
    g, r, c = lax.axis_index("groups"), lax.axis_index("row"), lax.axis_index("col")
    half = rows // 2
    tile, _, width = emb_ref.shape
    rim = tile // 2
    win = 2 * tile
    tok = win * win
    shard = wq_ref.shape[0]
    qkv = wq_ref.shape[1]
    hd = wo_ref.shape[1]
    head = hd // HEADS
    p = jnp.where(r % 2 == 0, r // 2, rows - 1 - r // 2)

    def row_at(position):
        q = lax.rem(position + 2 * rows, rows)
        return jnp.where(q < half, 2 * q, 2 * (rows - 1 - q) + 1)

    d = 1 - 2 * c
    ahead, behind = row_at(p + d), row_at(p - d)
    above, below = lax.rem(r + rows - 1, rows), lax.rem(r + 1, rows)
    other = 1 - c
    to_core, to_y = (g, r, other), (1 - g, r, c)

    names = {}

    def copy(name, src, dst, device):
        at = names.setdefault(name, len(names))
        return pltpu.make_async_remote_copy(
            src_ref=src, dst_ref=dst, send_sem=send_sems.at[at], recv_sem=recv_sems.at[at],
            device_id=device, device_id_type=MESH,
        )

    pending = []

    def start(name, src, dst, device):
        item = copy(name, src, dst, device)
        item.start()
        pending.append(item)

    def arrived(name, dst):
        copy(name, dst, dst, to_core).wait_recv()

    barrier = pltpu.get_barrier_semaphore()
    peers = [to_core, to_y, (g, ahead, c), (g, behind, c),
             (g, above, c), (g, below, c), (g, above, other), (g, below, other)]
    for peer in peers:
        pl.semaphore_signal(barrier, inc=1, device_id=peer, device_id_type=MESH)
    pl.semaphore_wait(barrier, len(peers))

    own_rows = pl.ds(rim, tile)
    halo_down = copy("hd", emb_ref.at[pl.ds(tile - rim, rim)], eb.at[0, pl.ds(0, rim)], (g, below, c))
    halo_up = copy("hu", emb_ref.at[pl.ds(0, rim)], eb.at[0, pl.ds(rim + tile, rim)], (g, above, c))

    @pl.when(r < rows - 1)
    def _():
        halo_down.start()

    @pl.when(r > 0)
    def _():
        halo_up.start()

    start("ec", emb_ref, eb.at[1, own_rows], to_core)
    start("v0", valid_ref, vb.at[0], (g, below, c))
    start("v2", valid_ref, vb.at[2], (g, above, c))
    start("v3", valid_ref, vb.at[3], (g, below, other))
    start("v4", valid_ref, vb.at[4], to_core)
    start("v5", valid_ref, vb.at[5], (g, above, other))

    class Stream:
        def __init__(self, name, ref, gathered):
            self.name, self.ref, self.all = name, ref, gathered
            units = ref.shape[1] // LANES
            side = (units + 1) // 3
            self.ring_w, self.y_w = (units - side) * LANES, side * LANES
            self.ring = pl.ds(pl.multiple_of(g * self.y_w, LANES), self.ring_w)
            self.y_out = pl.ds(pl.multiple_of(g * self.ring_w, LANES), self.y_w)
            self.y_in = pl.ds(pl.multiple_of((1 - g) * self.ring_w, LANES), self.y_w)

        def shard_row(self, way, step):
            return row_at(p - d * (step + 1)) if way == 0 else row_at(p + d * (step + 1))

        def place(self, row, core, cols):
            return self.all.at[row, core, :, cols]

        def send(self, way, step):
            row = r if step == 0 else self.shard_row(way, step - 1)
            src = self.ref.at[:, self.ring] if step == 0 else self.place(row, c, self.ring)
            device = (g, ahead if way == 0 else behind, c)
            start(f"{self.name}r{way}{step}", src, self.place(row, c, self.ring), device)

        def begin(self):
            self.send(0, 0)
            self.send(1, 0)

        def own(self):
            start(f"{self.name}o", self.ref, self.all.at[r, c], to_core)

        def ways(self, step):
            return (0, 1) if step < half - 1 else (0,)

        def ring_recv(self, step):
            for way in self.ways(step):
                row = self.shard_row(way, step)
                here = self.place(row, c, self.ring)
                arrived(f"{self.name}r{way}{step}", here)
                if way in self.ways(step + 1) and step + 1 < half:
                    self.send(way, step + 1)
                if step < half - 1:
                    side = self.place(row, c, self.y_out)
                    start(f"{self.name}y{way}{step}", side, side, to_y)
                start(f"{self.name}c{way}{step}", here, here, to_core)

        def y_recv(self, step):
            for way in self.ways(step):
                row = self.shard_row(way, step)
                here = self.place(row, c, self.y_in)
                if step < half - 1:
                    arrived(f"{self.name}y{way}{step}", here)
                    if step == half - 2 and way == 0:
                        start(f"{self.name}l", here, here, (g, ahead, c))
                else:
                    arrived(f"{self.name}l", here)
                start(f"{self.name}d{way}{step}", here, here, to_core)

        def core_recv(self, step):
            for way in self.ways(step):
                row = row_at(p + d * (step + 1)) if way == 0 else row_at(p - d * (step + 1))
                arrived(f"{self.name}c{way}{step}", self.place(row, other, self.ring))
                arrived(f"{self.name}d{way}{step}", self.place(row, other, self.y_in))

        def own_recv(self):
            arrived(f"{self.name}o", self.all.at[r, other])

    qs, ws = Stream("q", wq_ref, wq_all), Stream("w", wo_ref, wo_all)
    qs.begin()
    qs.own()
    ws.own()
    mine = [
        pltpu.make_async_copy(wq_ref, wq_all.at[r, c], local_sems.at[0]),
        pltpu.make_async_copy(wo_ref, wo_all.at[r, c], local_sems.at[1]),
    ]
    for item in mine:
        item.start()

    eb[0, rim:rim + tile] = emb_ref[...]

    @pl.when(r == 0)
    def _():
        eb[0, 0:rim] = jnp.zeros((rim, tile, width), eb.dtype)
        eb[1, 0:rim] = jnp.zeros((rim, tile, width), eb.dtype)

    @pl.when(r == rows - 1)
    def _():
        eb[0, rim + tile:] = jnp.zeros((rim, tile, width), eb.dtype)
        eb[1, rim + tile:] = jnp.zeros((rim, tile, width), eb.dtype)

    arrived("ec", eb.at[1, own_rows])
    fwd_top = copy("ft", eb.at[0, pl.ds(0, rim)], eb.at[1, pl.ds(0, rim)], to_core)
    fwd_bot = copy("fb", eb.at[0, pl.ds(rim + tile, rim)], eb.at[1, pl.ds(rim + tile, rim)], to_core)

    @pl.when(r > 0)
    def _():
        halo_down.wait_recv()
        fwd_top.start()

    @pl.when(r < rows - 1)
    def _():
        halo_up.wait_recv()
        fwd_bot.start()

    @pl.when(r > 0)
    def _():
        fwd_top.wait_recv()

    @pl.when(r < rows - 1)
    def _():
        fwd_bot.wait_recv()

    gain, bias = gain_ref[...], bias_ref[...]
    span = 2 * shard
    per = rim
    place = lax.broadcasted_iota(jnp.int32, (per, tile, 1), 1)
    rim_ok = jnp.where(c == 0, place, tile - 1 - place) < rim

    def norm_block(block, carry):
        at = pl.ds(block * per, per)
        left = eb[0, at].astype(jnp.float32)
        right = jnp.where(rim_ok, eb[1, at].astype(jnp.float32), 0.0)
        pos = pos_ref[pl.ds(pl.multiple_of(block * per * win, per * win), per * win)]
        pos = pos.astype(jnp.float32).reshape(per, win, width)
        pos = pltpu.roll(pos, win - rim, 1)
        posr[at] = pos
        x = (jnp.concatenate([left, right], axis=1) + pos).reshape(per * win, width)
        x = x - jnp.mean(x, axis=-1, keepdims=True)
        variance = jnp.mean(x * x, axis=-1, keepdims=True)
        x = x * lax.rsqrt(variance + EPSILON) * gain + bias
        there = pl.ds(pl.multiple_of(block * per * win, per * win), per * win)
        for k in range(rows):
            nrm[k, there] = x[:, k * span:(k + 1) * span].astype(jnp.bfloat16)
        return carry

    lax.fori_loop(0, win // per, norm_block, 0)

    for slot, name in ((0, "v0"), (2, "v2"), (3, "v3"), (4, "v4"), (5, "v5")):
        arrived(name, vb.at[slot])
    counts = [vb[0, 0], valid_ref[0], vb[2, 0], vb[3, 0], vb[4, 0], vb[5, 0]]
    counts = jnp.concatenate(
        [v.astype(jnp.float32) for v in counts] + [jnp.zeros((2, tok), jnp.float32)], axis=0
    ).astype(jnp.bfloat16)
    t_row = lax.broadcasted_iota(jnp.int32, (tok, tok), 0)
    t_col = lax.broadcasted_iota(jnp.int32, (tok, tok), 1)
    base_row = t_row // win * win
    pick = (t_col == base_row + (t_row - base_row + rim) % win).astype(jnp.float32).astype(jnp.bfloat16)
    counts = lax.dot_general(pick, counts, (((1,), (1,)), ((), ())), preferred_element_type=jnp.float32)
    t = lax.broadcasted_iota(jnp.int32, (tok, 1), 0)
    oi = (t // win).astype(jnp.float32) - (win - 1) / 2.0
    oj = ((t % win + rim) % win).astype(jnp.float32) - (win - 1) / 2.0
    gauss = jnp.exp(-(oi * oi + oj * oj) / (2.0 * SPREAD * SPREAD))
    weights = gauss * counts / 196.0
    wcol[...] = weights
    grid = weights.reshape(win, win, 8)
    near = grid[:, :tile].reshape(win * tile, 8)
    far = grid[:, tile:].reshape(win * tile, 8)
    u = lax.broadcasted_iota(jnp.int32, (win * tile, 1), 0) % tile
    fold_ok = jnp.where(c == 1, u, tile - 1 - u) < rim
    far = jnp.where(fold_ok, far, 0.0)
    low, high = rim * tile, (rim + tile) * tile
    has_above, has_below = r > 0, r < rows - 1
    near0, far0 = near[low:high, 1:2], far[low:high, 4:5]
    near_a = jnp.where(has_above, near[high:, 0:1], 0.0)
    far_a = jnp.where(has_above, far[high:, 3:4], 0.0)
    near_b = jnp.where(has_below, near[:low, 2:3], 0.0)
    far_b = jnp.where(has_below, far[:low, 5:6], 0.0)
    denom = near0 + far0 + jnp.concatenate([near_a + far_a, near_b + far_b], axis=0)

    qs.ring_recv(0)
    ws.begin()

    def flat(lo, hi, a, b):
        return posr[lo:hi, a:b].reshape((hi - lo) * (b - a), width)

    total = denom * (emb_ref[...].astype(jnp.float32).reshape(tile * tile, width) + bo_ref[...])
    total += near0 * flat(rim, rim + tile, 0, tile) + far0 * flat(rim, rim + tile, tile, win)
    base[...] = total
    base[0:low] += near_a * flat(rim + tile, win, 0, tile) + far_a * flat(rim + tile, win, tile, win)
    base[low:] += near_b * flat(0, rim, 0, tile) + far_b * flat(0, rim, tile, win)

    block_n = qkv // 3

    def multiply(row, first=False):
        def part(n, carry):
            cols = pl.ds(pl.multiple_of(n * block_n, LANES), block_n)
            got = jnp.dot(
                nrm[row], wq_all[row, :, :, cols].reshape(span, block_n),
                preferred_element_type=jnp.float32,
            )
            if first:
                proj[:, cols] = got + bq_ref[:, cols]
            else:
                proj[:, cols] += got
            return carry

        lax.fori_loop(0, 3, part, 0)

    for item in mine:
        item.wait()
    qs.own_recv()
    multiply(r, True)

    for step in range(1, half):
        last = step == half - 1
        if not last:
            qs.ring_recv(step)
        qs.y_recv(step - 1)
        qs.core_recv(step - 1)
        multiply(row_at(p - step))
        multiply(row_at(p + step))
        if last:
            qs.ring_recv(step)
        ws.ring_recv(step - 1)
        if step >= 2:
            ws.y_recv(step - 2)
    qs.y_recv(half - 1)
    qs.core_recv(half - 1)
    multiply(row_at(p + half))

    def attend(h):
        lo, hi = h * head, (h + 1) * head
        a, b = lo // LANES * LANES, -(-hi // LANES) * LANES
        lane = lax.broadcasted_iota(jnp.int32, (1, b - a), 1) + a
        inside = (lane >= lo) & (lane < hi)
        q = jnp.where(inside, proj[:, a:b], 0.0).astype(jnp.bfloat16)
        k = proj[:, hd + a:hd + b].astype(jnp.bfloat16)
        v = proj[:, 2 * hd + a:2 * hd + b].astype(jnp.bfloat16)
        scores = lax.dot_general(
            q, k, (((1,), (1,)), ((), ())), preferred_element_type=jnp.float32
        ) * head ** (-0.5)
        expon = jnp.exp(scores - jnp.max(scores, axis=-1, keepdims=True))
        probs = (expon / jnp.sum(expon, axis=-1, keepdims=True)).astype(jnp.bfloat16)
        mixed = jnp.dot(probs, v, preferred_element_type=jnp.float32)
        att[:, a:b] = mixed if lo == a else jnp.where(inside, mixed, att[:, a:b])

    for h in range(HEADS // 2):
        attend(h)
    ws.y_recv(half - 2)
    for h in range(HEADS // 2, HEADS):
        attend(h)
    ws.ring_recv(half - 1)

    merged = att[...].astype(jnp.bfloat16).astype(jnp.float32) * wcol[:, 1:2]
    merged = merged.reshape(win, win, hd)
    rim_out[...] = merged[:, tile:].reshape(win * tile, hd).astype(jnp.bfloat16)
    start("rc", rim_out, rim_in, to_core)
    own = merged[:, :tile].reshape(win * tile, hd)
    ws.y_recv(half - 1)
    arrived("rc", rim_in)
    own = own + jnp.where(fold_ok, rim_in[...].astype(jnp.float32), 0.0)
    top_out[...] = own[:low].astype(jnp.bfloat16)
    bot_out[...] = own[high:].astype(jnp.bfloat16)
    send_top = copy("rt", top_out, bot_in, (g, above, c))
    send_bot = copy("rb", bot_out, top_in, (g, below, c))

    @pl.when(r > 0)
    def _():
        send_top.start()

    @pl.when(r < rows - 1)
    def _():
        send_bot.start()

    @pl.when(r == 0)
    def _():
        top_in[...] = jnp.zeros_like(top_in)

    @pl.when(r == rows - 1)
    def _():
        bot_in[...] = jnp.zeros_like(bot_in)

    for step in range(half):
        ws.core_recv(step)
    ws.own_recv()

    @pl.when(r > 0)
    def _():
        send_bot.wait_recv()

    @pl.when(r < rows - 1)
    def _():
        send_top.wait_recv()

    own = own[low:high] + jnp.concatenate(
        [top_in[...].astype(jnp.float32), bot_in[...].astype(jnp.float32)], axis=0
    )
    result = base[...] + lax.dot_general(
        own.astype(jnp.bfloat16), wo_all[...].reshape(width, hd),
        (((1,), (1,)), ((), ())), preferred_element_type=jnp.float32,
    )
    result = result / jnp.maximum(denom, FLOOR)
    out_ref[...] = result.reshape(tile, tile, width).astype(out_ref.dtype)

    for item in pending:
        item.wait_send()

    @pl.when(r > 0)
    def _():
        halo_up.wait_send()
        fwd_top.wait_send()
        send_top.wait_send()

    @pl.when(r < rows - 1)
    def _():
        halo_down.wait_send()
        fwd_bot.wait_send()
        send_bot.wait_send()


def fused(rows, embeddings, pos_embed, ln_gain, ln_bias, w_qkv, b_qkv, w_out, b_out, valid):
    tile, _, width = embeddings.shape
    win, rim = 2 * tile, tile // 2
    tok = win * win
    shard, qkv = w_qkv.shape
    hd = w_out.shape[1]
    copies = 8 * 8 * rows
    bf16, f32 = jnp.bfloat16, jnp.float32
    vmem = pl.BlockSpec(memory_space=pltpu.VMEM)
    return pl.pallas_call(
        functools.partial(kernel, rows),
        out_shape=jax.ShapeDtypeStruct(embeddings.shape, bf16),
        in_specs=[vmem] * 9,
        out_specs=vmem,
        scratch_shapes=[
            pltpu.VMEM((2, win, tile, width), bf16),
            pltpu.VMEM((6, 1, 1, tok), jnp.int32),
            pltpu.VMEM((rows, 2, shard, qkv), bf16),
            pltpu.VMEM((rows, 2, shard, hd), bf16),
            pltpu.VMEM((rows, tok, 2 * shard), bf16),
            pltpu.VMEM((tok, qkv), f32),
            pltpu.VMEM((win, win, width), f32),
            pltpu.VMEM((tile * tile, width), f32),
            pltpu.VMEM((tok, 8), f32),
            pltpu.VMEM((tok, hd), f32),
            pltpu.VMEM((win * tile, hd), bf16),
            pltpu.VMEM((win * tile, hd), bf16),
            pltpu.VMEM((rim * tile, hd), bf16),
            pltpu.VMEM((rim * tile, hd), bf16),
            pltpu.VMEM((rim * tile, hd), bf16),
            pltpu.VMEM((rim * tile, hd), bf16),
            pltpu.SemaphoreType.DMA((96,)),
            pltpu.SemaphoreType.DMA((96,)),
            pltpu.SemaphoreType.DMA((2,)),
        ],
        compiler_params=pltpu.CompilerParams(
            collective_id=0, has_side_effects=True, vmem_limit_bytes=48 * 1024 * 1024
        ),
    )(
        embeddings, pos_embed, ln_gain.reshape(1, -1), ln_bias.reshape(1, -1), w_qkv,
        b_qkv.reshape(1, -1), w_out, b_out.reshape(1, -1), valid,
    )


def shifted(value, axis, steps):
    count = lax.axis_size(axis)
    initial, last = (max(0, -steps), min(count, count - steps))
    return lax.ppermute(value, axis, [(source, source + steps) for source in range(initial, last)])


def extended(block, sides, width):
    for axis, dim in sides:
        count = lax.axis_size(axis)
        forward = [(i, i + 1) for i in range(count - 1)]
        backward = [(target, source) for source, target in forward]
        low = lax.ppermute(
            lax.slice_in_dim(block, block.shape[dim] - width, None, axis=dim), axis, forward
        )
        high = lax.ppermute(lax.slice_in_dim(block, 0, width, axis=dim), axis, backward)
        block = jnp.concatenate([low, block, high], axis=dim)
    return block


def layer_norm(inputs, ln_gain, ln_bias):
    centred = inputs - jnp.mean(inputs, axis=-1, keepdims=True)
    variance = jnp.mean(centred * centred, axis=-1, keepdims=True)
    return centred * lax.rsqrt(variance + EPSILON) * ln_gain + ln_bias


def gauss_table(win):
    offsets = jnp.arange(win, dtype=jnp.float32) - (win - 1) / 2.0
    squared = offsets[:, None] * offsets[:, None] + offsets[None, :] * offsets[None, :]
    return jnp.exp(-squared / (2.0 * SPREAD * SPREAD))


def attend(projected):
    rows_count = projected.shape[0]
    width = projected.shape[1] // 3
    head_size = width // HEADS
    queries = projected[:, :width].reshape(rows_count, HEADS, head_size)
    keys = projected[:, width : 2 * width].reshape(rows_count, HEADS, head_size)
    values = projected[:, 2 * width :].reshape(rows_count, HEADS, head_size)
    scores = jnp.einsum(
        "qhd,khd->hqk", queries, keys, preferred_element_type=jnp.float32
    ) * head_size ** (-0.5)
    highest = jnp.max(scores, axis=-1, keepdims=True)
    expon = jnp.exp(scores - highest)
    probs = (expon / jnp.sum(expon, axis=-1, keepdims=True)).astype(jnp.bfloat16)
    mixed = jnp.einsum("hqk,khd->qhd", probs, values, preferred_element_type=jnp.float32)
    return mixed.astype(jnp.bfloat16).reshape(rows_count, width)


def fold_rows(numerator, denominator, rim):
    from_next = (
        shifted(numerator[:rim].astype(jnp.bfloat16), "row", -1).astype(jnp.float32),
        shifted(denominator[:rim].astype(jnp.bfloat16), "row", -1).astype(jnp.float32),
    )
    from_prev = (
        shifted(numerator[-rim:].astype(jnp.bfloat16), "row", 1).astype(jnp.float32),
        shifted(denominator[-rim:].astype(jnp.bfloat16), "row", 1).astype(jnp.float32),
    )
    middle_num = numerator[rim:-rim]
    middle_den = denominator[rim:-rim]
    middle_num = middle_num.at[:rim].add(from_prev[0]).at[-rim:].add(from_next[0])
    middle_den = middle_den.at[:rim].add(from_prev[1]).at[-rim:].add(from_next[1])
    return (middle_num, middle_den)


def fold_cols(numerator, denominator, rim):
    from_next = (
        shifted(numerator[:, :rim].astype(jnp.bfloat16), "col", -1).astype(jnp.float32),
        shifted(denominator[:, :rim].astype(jnp.bfloat16), "col", -1).astype(jnp.float32),
    )
    from_prev = (
        shifted(numerator[:, -rim:].astype(jnp.bfloat16), "col", 1).astype(jnp.float32),
        shifted(denominator[:, -rim:].astype(jnp.bfloat16), "col", 1).astype(jnp.float32),
    )
    middle_num = numerator[:, rim:-rim] + jnp.concatenate([from_prev[0], from_next[0]], axis=1)
    middle_den = denominator[:, rim:-rim] + jnp.concatenate([from_prev[1], from_next[1]], axis=1)
    return (middle_num, middle_den)


def body(embeddings, pos_embed, ln_gain, ln_bias, w_qkv, b_qkv, w_out, b_out, valid):
    tile = embeddings.shape[1]
    tile_rows = embeddings.shape[0] // tile
    rim = tile // 2
    win = tile + 2 * rim
    rows_count = win * win
    width_model = embeddings.shape[2]
    window = extended(embeddings, (("row", 0), ("col", 1)), rim)
    stacked = jnp.stack([window], axis=0)
    inputs = stacked.reshape(tile_rows, rows_count, width_model).astype(
        jnp.float32
    ) + pos_embed.astype(jnp.float32)
    inputs = inputs.reshape(tile_rows * rows_count, width_model)
    normed = layer_norm(inputs, ln_gain, ln_bias).astype(jnp.bfloat16)
    projected = jnp.dot(
        normed,
        lax.all_gather(w_qkv, ("row", "col"), axis=0, tiled=True),
        preferred_element_type=jnp.float32,
    )
    projected = (
        (projected + b_qkv).astype(jnp.bfloat16).reshape(tile_rows, rows_count, w_qkv.shape[1])
    )
    attended = jax.vmap(attend)(projected).reshape(tile_rows * rows_count, -1)
    projected_out = lax.dot_general(
        attended,
        lax.all_gather(w_out, ("row", "col"), axis=0, tiled=True),
        (((1,), (1,)), ((), ())),
        preferred_element_type=jnp.float32,
    )
    hidden = inputs + projected_out + b_out
    gauss = gauss_table(win).reshape(1, rows_count)
    weight = gauss * valid.reshape(tile_rows, rows_count).astype(jnp.float32) / 196.0
    contrib = (weight.reshape(tile_rows * rows_count, 1) * hidden).reshape(
        tile_rows, win, win, width_model
    )
    weight_grid = weight.reshape(tile_rows, win, win)
    numerator = jnp.zeros((tile_rows * tile + 2 * rim, win, width_model), jnp.float32)
    denominator = jnp.zeros((tile_rows * tile + 2 * rim, win), jnp.float32)
    numerator = numerator.at[0:win].add(contrib[0])
    denominator = denominator.at[0:win].add(weight_grid[0])
    numerator, denominator = fold_rows(numerator, denominator, rim)
    numerator, denominator = fold_cols(numerator, denominator, rim)
    return (numerator / jnp.maximum(denominator, FLOOR)[:, :, None]).astype(jnp.bfloat16)


def solution(mesh):
    placed = (
        P(("groups", "row"), "col", None),
        P(),
        P(),
        P(),
        P(("row", "col"), None),
        P(),
        P(("row", "col"), None),
        P(),
        P(("groups", "row"), "col", None),
    )
    rows = mesh.shape["row"]

    def run(*arrays):
        embeddings, w_qkv = arrays[0], arrays[4]
        tile = embeddings.shape[1]
        whole_tiles = w_qkv.shape[0] % 16 == 0 and embeddings.shape[0] == tile == 8
        pairs = mesh.shape["groups"] == 2 and mesh.shape["col"] == 2
        if whole_tiles and pairs and rows == 8:
            return fused(rows, *arrays)
        return body(*arrays)

    return jax.shard_map(
        run,
        mesh=mesh,
        in_specs=placed,
        out_specs=P(("groups", "row"), "col", None),
        check_vma=False,
    )
```

```python
import functools

import jax
import jax.numpy as jnp
from jax import lax
from jax.experimental import pallas as pl
from jax.experimental.pallas import tpu as pltpu
from jax.sharding import PartitionSpec as P

HEADS = 8
EPSILON = 1e-06
SPREAD = 4.0
FLOOR = 0.25
LANES = 128
MESH = pl.DeviceIdType.MESH


def kernel(
    rows,
    emb_ref, pos_hbm, gain_hbm, bias_hbm, wq_ref, bq_hbm, wo_ref, bo_hbm, valid_ref,
    out_ref, pos_ref, gain_ref, bias_ref, bq_ref, bo_ref,
    eb, vb, wq_all, wo_all, nrm, proj, posr, base, wcol, att, rim_out, rim_in,
    top_out, top_in, bot_out, bot_in, send_sems, recv_sems, local_sems,
):
    g, r, c = lax.axis_index("groups"), lax.axis_index("row"), lax.axis_index("col")
    half = rows // 2
    tile, _, width = emb_ref.shape
    rim = tile // 2
    win = 2 * tile
    tok = win * win
    shard = wq_ref.shape[0]
    qkv = wq_ref.shape[1]
    hd = wo_ref.shape[1]
    head = hd // HEADS
    p = jnp.where(r % 2 == 0, r // 2, rows - 1 - r // 2)

    def row_at(position):
        q = lax.rem(position + 2 * rows, rows)
        return jnp.where(q < half, 2 * q, 2 * (rows - 1 - q) + 1)

    d = 1 - 2 * c
    ahead, behind = row_at(p + d), row_at(p - d)
    above, below = lax.rem(r + rows - 1, rows), lax.rem(r + 1, rows)
    other = 1 - c
    to_core, to_y = (g, r, other), (1 - g, r, c)

    names = {}

    def copy(name, src, dst, device):
        at = names.setdefault(name, len(names))
        return pltpu.make_async_remote_copy(
            src_ref=src, dst_ref=dst, send_sem=send_sems.at[at], recv_sem=recv_sems.at[at],
            device_id=device, device_id_type=MESH,
        )

    pending = []

    def start(name, src, dst, device):
        item = copy(name, src, dst, device)
        item.start()
        pending.append(item)

    def arrived(name, dst):
        copy(name, dst, dst, to_core).wait_recv()

    own_rows = pl.ds(tile // 2, tile)
    locals_ = []
    for src, dst in (
        (emb_ref, eb.at[0, own_rows]), (valid_ref, vb.at[1]), (pos_hbm, pos_ref),
        (gain_hbm, gain_ref), (bias_hbm, bias_ref), (bo_hbm, bo_ref), (bq_hbm, bq_ref),
        (wq_ref, wq_all.at[r, c]), (wo_ref, wo_all.at[r, c]),
    ):
        item = pltpu.make_async_copy(src, dst, local_sems.at[len(locals_)])
        item.start()
        locals_.append(item)

    barrier = pltpu.get_barrier_semaphore()
    peers = [to_core, to_y, (g, ahead, c), (g, behind, c),
             (g, above, c), (g, below, c), (g, above, other), (g, below, other)]
    for peer in peers:
        pl.semaphore_signal(barrier, inc=1, device_id=peer, device_id_type=MESH)
    pl.semaphore_wait(barrier, len(peers))

    halo_down = copy("hd", emb_ref.at[pl.ds(tile - rim, rim)], eb.at[0, pl.ds(0, rim)], (g, below, c))
    halo_up = copy("hu", emb_ref.at[pl.ds(0, rim)], eb.at[0, pl.ds(rim + tile, rim)], (g, above, c))

    @pl.when(r < rows - 1)
    def _():
        halo_down.start()

    @pl.when(r > 0)
    def _():
        halo_up.start()

    start("ec", emb_ref, eb.at[1, own_rows], to_core)
    start("v0", valid_ref, vb.at[0], (g, below, c))
    start("v2", valid_ref, vb.at[2], (g, above, c))
    start("v3", valid_ref, vb.at[3], (g, below, other))
    start("v4", valid_ref, vb.at[4], to_core)
    start("v5", valid_ref, vb.at[5], (g, above, other))

    class Stream:
        def __init__(self, name, ref, gathered):
            self.name, self.ref, self.all = name, ref, gathered
            units = ref.shape[1] // LANES
            side = (units + 1) // 3
            self.ring_w, self.y_w = (units - side) * LANES, side * LANES
            self.ring = pl.ds(pl.multiple_of(g * self.y_w, LANES), self.ring_w)
            self.y_out = pl.ds(pl.multiple_of(g * self.ring_w, LANES), self.y_w)
            self.y_in = pl.ds(pl.multiple_of((1 - g) * self.ring_w, LANES), self.y_w)

        def shard_row(self, way, step):
            return row_at(p - d * (step + 1)) if way == 0 else row_at(p + d * (step + 1))

        def place(self, row, core, cols):
            return self.all.at[row, core, :, cols]

        def send(self, way, step):
            row = r if step == 0 else self.shard_row(way, step - 1)
            src = self.ref.at[:, self.ring] if step == 0 else self.place(row, c, self.ring)
            device = (g, ahead if way == 0 else behind, c)
            start(f"{self.name}r{way}{step}", src, self.place(row, c, self.ring), device)

        def begin(self):
            self.send(0, 0)
            self.send(1, 0)

        def own(self):
            start(f"{self.name}o", self.ref, self.all.at[r, c], to_core)

        def ways(self, step):
            return (0, 1) if step < half - 1 else (0,)

        def ring_recv(self, step):
            for way in self.ways(step):
                row = self.shard_row(way, step)
                here = self.place(row, c, self.ring)
                arrived(f"{self.name}r{way}{step}", here)
                if way in self.ways(step + 1) and step + 1 < half:
                    self.send(way, step + 1)
                if step < half - 1:
                    side = self.place(row, c, self.y_out)
                    start(f"{self.name}y{way}{step}", side, side, to_y)
                start(f"{self.name}c{way}{step}", here, here, to_core)

        def y_recv(self, step):
            for way in self.ways(step):
                row = self.shard_row(way, step)
                here = self.place(row, c, self.y_in)
                if step < half - 1:
                    arrived(f"{self.name}y{way}{step}", here)
                    if step == half - 2 and way == 0:
                        start(f"{self.name}l", here, here, (g, ahead, c))
                else:
                    arrived(f"{self.name}l", here)
                start(f"{self.name}d{way}{step}", here, here, to_core)

        def core_recv(self, step):
            for way in self.ways(step):
                row = row_at(p + d * (step + 1)) if way == 0 else row_at(p - d * (step + 1))
                arrived(f"{self.name}c{way}{step}", self.place(row, other, self.ring))
                arrived(f"{self.name}d{way}{step}", self.place(row, other, self.y_in))

        def own_recv(self):
            arrived(f"{self.name}o", self.all.at[r, other])

    qs, ws = Stream("q", wq_ref, wq_all), Stream("w", wo_ref, wo_all)
    qs.begin()
    qs.own()
    ws.own()

    @pl.when(r == 0)
    def _():
        eb[0, 0:rim] = jnp.zeros((rim, tile, width), eb.dtype)
        eb[1, 0:rim] = jnp.zeros((rim, tile, width), eb.dtype)

    @pl.when(r == rows - 1)
    def _():
        eb[0, rim + tile:] = jnp.zeros((rim, tile, width), eb.dtype)
        eb[1, rim + tile:] = jnp.zeros((rim, tile, width), eb.dtype)

    arrived("ec", eb.at[1, own_rows])
    fwd_top = copy("ft", eb.at[0, pl.ds(0, rim)], eb.at[1, pl.ds(0, rim)], to_core)
    fwd_bot = copy("fb", eb.at[0, pl.ds(rim + tile, rim)], eb.at[1, pl.ds(rim + tile, rim)], to_core)

    @pl.when(r > 0)
    def _():
        halo_down.wait_recv()
        fwd_top.start()

    @pl.when(r < rows - 1)
    def _():
        halo_up.wait_recv()
        fwd_bot.start()

    @pl.when(r > 0)
    def _():
        fwd_top.wait_recv()

    @pl.when(r < rows - 1)
    def _():
        fwd_bot.wait_recv()

    for item in locals_[:6]:
        item.wait()
    gain, bias = gain_ref[...].reshape(1, width), bias_ref[...].reshape(1, width)
    span = 2 * shard
    per = rim
    place = lax.broadcasted_iota(jnp.int32, (per, tile, 1), 1)
    rim_ok = jnp.where(c == 0, place, tile - 1 - place) < rim

    def norm_block(block, carry):
        at = pl.ds(block * per, per)
        left = eb[0, at].astype(jnp.float32)
        right = jnp.where(rim_ok, eb[1, at].astype(jnp.float32), 0.0)
        pos = pos_ref[pl.ds(pl.multiple_of(block * per * win, per * win), per * win)]
        pos = pos.astype(jnp.float32).reshape(per, win, width)
        pos = pltpu.roll(pos, win - rim, 1)
        posr[at] = pos
        x = (jnp.concatenate([left, right], axis=1) + pos).reshape(per * win, width)
        x = x - jnp.mean(x, axis=-1, keepdims=True)
        variance = jnp.mean(x * x, axis=-1, keepdims=True)
        x = x * lax.rsqrt(variance + EPSILON) * gain + bias
        there = pl.ds(pl.multiple_of(block * per * win, per * win), per * win)
        for k in range(rows):
            nrm[k, there] = x[:, k * span:(k + 1) * span].astype(jnp.bfloat16)
        return carry

    lax.fori_loop(0, win // per, norm_block, 0)

    for slot, name in ((0, "v0"), (2, "v2"), (3, "v3"), (4, "v4"), (5, "v5")):
        arrived(name, vb.at[slot])
    counts = [vb[0, 0], vb[1, 0], vb[2, 0], vb[3, 0], vb[4, 0], vb[5, 0]]
    counts = jnp.concatenate(
        [v.astype(jnp.float32) for v in counts] + [jnp.zeros((2, tok), jnp.float32)], axis=0
    ).astype(jnp.bfloat16)
    t_row = lax.broadcasted_iota(jnp.int32, (tok, tok), 0)
    t_col = lax.broadcasted_iota(jnp.int32, (tok, tok), 1)
    base_row = t_row // win * win
    pick = (t_col == base_row + (t_row - base_row + rim) % win).astype(jnp.float32).astype(jnp.bfloat16)
    counts = lax.dot_general(pick, counts, (((1,), (1,)), ((), ())), preferred_element_type=jnp.float32)
    t = lax.broadcasted_iota(jnp.int32, (tok, 1), 0)
    oi = (t // win).astype(jnp.float32) - (win - 1) / 2.0
    oj = ((t % win + rim) % win).astype(jnp.float32) - (win - 1) / 2.0
    gauss = jnp.exp(-(oi * oi + oj * oj) / (2.0 * SPREAD * SPREAD))
    weights = gauss * counts / 196.0
    wcol[...] = weights
    grid = weights.reshape(win, win, 8)
    near = grid[:, :tile].reshape(win * tile, 8)
    far = grid[:, tile:].reshape(win * tile, 8)
    u = lax.broadcasted_iota(jnp.int32, (win * tile, 1), 0) % tile
    fold_ok = jnp.where(c == 1, u, tile - 1 - u) < rim
    far = jnp.where(fold_ok, far, 0.0)
    low, high = rim * tile, (rim + tile) * tile
    has_above, has_below = r > 0, r < rows - 1
    near0, far0 = near[low:high, 1:2], far[low:high, 4:5]
    near_a = jnp.where(has_above, near[high:, 0:1], 0.0)
    far_a = jnp.where(has_above, far[high:, 3:4], 0.0)
    near_b = jnp.where(has_below, near[:low, 2:3], 0.0)
    far_b = jnp.where(has_below, far[:low, 5:6], 0.0)
    denom = near0 + far0 + jnp.concatenate([near_a + far_a, near_b + far_b], axis=0)

    qs.ring_recv(0)
    ws.begin()

    def flat(lo, hi, a, b):
        return posr[lo:hi, a:b].reshape((hi - lo) * (b - a), width)

    total = denom * (
        eb[0, rim:rim + tile].astype(jnp.float32).reshape(tile * tile, width)
        + bo_ref[...].reshape(1, width)
    )
    total += near0 * flat(rim, rim + tile, 0, tile) + far0 * flat(rim, rim + tile, tile, win)
    base[...] = total
    base[0:low] += near_a * flat(rim + tile, win, 0, tile) + far_a * flat(rim + tile, win, tile, win)
    base[low:] += near_b * flat(0, rim, 0, tile) + far_b * flat(0, rim, tile, win)

    block_n = qkv // 3

    def multiply(row, first=False):
        def part(n, carry):
            cols = pl.ds(pl.multiple_of(n * block_n, LANES), block_n)
            got = jnp.dot(
                nrm[row], wq_all[row, :, :, cols].reshape(span, block_n),
                preferred_element_type=jnp.float32,
            )
            if first:
                proj[:, cols] = got + bq_ref[cols].reshape(1, block_n)
            else:
                proj[:, cols] += got
            return carry

        lax.fori_loop(0, 3, part, 0)

    for item in locals_[6:]:
        item.wait()
    qs.own_recv()
    multiply(r, True)

    for step in range(1, half):
        last = step == half - 1
        if not last:
            qs.ring_recv(step)
        qs.y_recv(step - 1)
        qs.core_recv(step - 1)
        multiply(row_at(p - step))
        multiply(row_at(p + step))
        if last:
            qs.ring_recv(step)
        ws.ring_recv(step - 1)
        if step >= 2:
            ws.y_recv(step - 2)
    qs.y_recv(half - 1)
    qs.core_recv(half - 1)
    multiply(row_at(p + half))

    def attend(h):
        lo, hi = h * head, (h + 1) * head
        a, b = lo // LANES * LANES, -(-hi // LANES) * LANES
        lane = lax.broadcasted_iota(jnp.int32, (1, b - a), 1) + a
        inside = (lane >= lo) & (lane < hi)
        q = jnp.where(inside, proj[:, a:b], 0.0).astype(jnp.bfloat16)
        k = proj[:, hd + a:hd + b].astype(jnp.bfloat16)
        v = proj[:, 2 * hd + a:2 * hd + b].astype(jnp.bfloat16)
        scores = lax.dot_general(
            q, k, (((1,), (1,)), ((), ())), preferred_element_type=jnp.float32
        ) * head ** (-0.5)
        expon = jnp.exp(scores - jnp.max(scores, axis=-1, keepdims=True))
        probs = (expon / jnp.sum(expon, axis=-1, keepdims=True)).astype(jnp.bfloat16)
        mixed = jnp.dot(probs, v, preferred_element_type=jnp.float32)
        att[:, a:b] = mixed if lo == a else jnp.where(inside, mixed, att[:, a:b])

    for h in range(HEADS // 2):
        attend(h)
    ws.y_recv(half - 2)
    for h in range(HEADS // 2, HEADS):
        attend(h)
    ws.ring_recv(half - 1)

    merged = att[...].astype(jnp.bfloat16).astype(jnp.float32) * wcol[:, 1:2]
    merged = merged.reshape(win, win, hd)
    rim_out[...] = merged[:, tile:].reshape(win * tile, hd).astype(jnp.bfloat16)
    start("rc", rim_out, rim_in, to_core)
    own = merged[:, :tile].reshape(win * tile, hd)
    ws.y_recv(half - 1)
    arrived("rc", rim_in)
    own = own + jnp.where(fold_ok, rim_in[...].astype(jnp.float32), 0.0)
    top_out[...] = own[:low].astype(jnp.bfloat16)
    bot_out[...] = own[high:].astype(jnp.bfloat16)
    send_top = copy("rt", top_out, bot_in, (g, above, c))
    send_bot = copy("rb", bot_out, top_in, (g, below, c))

    @pl.when(r > 0)
    def _():
        send_top.start()

    @pl.when(r < rows - 1)
    def _():
        send_bot.start()

    @pl.when(r == 0)
    def _():
        top_in[...] = jnp.zeros_like(top_in)

    @pl.when(r == rows - 1)
    def _():
        bot_in[...] = jnp.zeros_like(bot_in)

    for step in range(half):
        ws.core_recv(step)
    ws.own_recv()

    @pl.when(r > 0)
    def _():
        send_bot.wait_recv()

    @pl.when(r < rows - 1)
    def _():
        send_top.wait_recv()

    own = own[low:high] + jnp.concatenate(
        [top_in[...].astype(jnp.float32), bot_in[...].astype(jnp.float32)], axis=0
    )
    result = base[...] + lax.dot_general(
        own.astype(jnp.bfloat16), wo_all[...].reshape(width, hd),
        (((1,), (1,)), ((), ())), preferred_element_type=jnp.float32,
    )
    result = result / jnp.maximum(denom, FLOOR)
    out_ref[...] = result.reshape(tile, tile, width).astype(out_ref.dtype)

    for item in pending:
        item.wait_send()

    @pl.when(r > 0)
    def _():
        halo_up.wait_send()
        fwd_top.wait_send()
        send_top.wait_send()

    @pl.when(r < rows - 1)
    def _():
        halo_down.wait_send()
        fwd_bot.wait_send()
        send_bot.wait_send()


def fused(rows, embeddings, pos_embed, ln_gain, ln_bias, w_qkv, b_qkv, w_out, b_out, valid):
    tile, _, width = embeddings.shape
    win, rim = 2 * tile, tile // 2
    tok = win * win
    shard, qkv = w_qkv.shape
    hd = w_out.shape[1]
    copies = 8 * 8 * rows
    bf16, f32 = jnp.bfloat16, jnp.float32
    vmem = pl.BlockSpec(memory_space=pltpu.VMEM)
    return pl.pallas_call(
        functools.partial(kernel, rows),
        out_shape=jax.ShapeDtypeStruct(embeddings.shape, bf16),
        in_specs=[pl.BlockSpec(memory_space=pltpu.HBM)] * 9,
        out_specs=vmem,
        scratch_shapes=[
            pltpu.VMEM((tok, width), bf16),
            pltpu.VMEM((width,), f32),
            pltpu.VMEM((width,), f32),
            pltpu.VMEM((qkv,), f32),
            pltpu.VMEM((width,), f32),
            pltpu.VMEM((2, win, tile, width), bf16),
            pltpu.VMEM((6, 1, 1, tok), jnp.int32),
            pltpu.VMEM((rows, 2, shard, qkv), bf16),
            pltpu.VMEM((rows, 2, shard, hd), bf16),
            pltpu.VMEM((rows, tok, 2 * shard), bf16),
            pltpu.VMEM((tok, qkv), f32),
            pltpu.VMEM((win, win, width), f32),
            pltpu.VMEM((tile * tile, width), f32),
            pltpu.VMEM((tok, 8), f32),
            pltpu.VMEM((tok, hd), f32),
            pltpu.VMEM((win * tile, hd), bf16),
            pltpu.VMEM((win * tile, hd), bf16),
            pltpu.VMEM((rim * tile, hd), bf16),
            pltpu.VMEM((rim * tile, hd), bf16),
            pltpu.VMEM((rim * tile, hd), bf16),
            pltpu.VMEM((rim * tile, hd), bf16),
            pltpu.SemaphoreType.DMA((96,)),
            pltpu.SemaphoreType.DMA((96,)),
            pltpu.SemaphoreType.DMA((9,)),
        ],
        compiler_params=pltpu.CompilerParams(
            collective_id=0, has_side_effects=True, vmem_limit_bytes=67043328
        ),
    )(
        embeddings, pos_embed, ln_gain, ln_bias, w_qkv, b_qkv, w_out, b_out, valid
    )


def shifted(value, axis, steps):
    count = lax.axis_size(axis)
    initial, last = (max(0, -steps), min(count, count - steps))
    return lax.ppermute(value, axis, [(source, source + steps) for source in range(initial, last)])


def extended(block, sides, width):
    for axis, dim in sides:
        count = lax.axis_size(axis)
        forward = [(i, i + 1) for i in range(count - 1)]
        backward = [(target, source) for source, target in forward]
        low = lax.ppermute(
            lax.slice_in_dim(block, block.shape[dim] - width, None, axis=dim), axis, forward
        )
        high = lax.ppermute(lax.slice_in_dim(block, 0, width, axis=dim), axis, backward)
        block = jnp.concatenate([low, block, high], axis=dim)
    return block


def layer_norm(inputs, ln_gain, ln_bias):
    centred = inputs - jnp.mean(inputs, axis=-1, keepdims=True)
    variance = jnp.mean(centred * centred, axis=-1, keepdims=True)
    return centred * lax.rsqrt(variance + EPSILON) * ln_gain + ln_bias


def gauss_table(win):
    offsets = jnp.arange(win, dtype=jnp.float32) - (win - 1) / 2.0
    squared = offsets[:, None] * offsets[:, None] + offsets[None, :] * offsets[None, :]
    return jnp.exp(-squared / (2.0 * SPREAD * SPREAD))


def attend(projected):
    rows_count = projected.shape[0]
    width = projected.shape[1] // 3
    head_size = width // HEADS
    queries = projected[:, :width].reshape(rows_count, HEADS, head_size)
    keys = projected[:, width : 2 * width].reshape(rows_count, HEADS, head_size)
    values = projected[:, 2 * width :].reshape(rows_count, HEADS, head_size)
    scores = jnp.einsum(
        "qhd,khd->hqk", queries, keys, preferred_element_type=jnp.float32
    ) * head_size ** (-0.5)
    highest = jnp.max(scores, axis=-1, keepdims=True)
    expon = jnp.exp(scores - highest)
    probs = (expon / jnp.sum(expon, axis=-1, keepdims=True)).astype(jnp.bfloat16)
    mixed = jnp.einsum("hqk,khd->qhd", probs, values, preferred_element_type=jnp.float32)
    return mixed.astype(jnp.bfloat16).reshape(rows_count, width)


def fold_rows(numerator, denominator, rim):
    from_next = (
        shifted(numerator[:rim].astype(jnp.bfloat16), "row", -1).astype(jnp.float32),
        shifted(denominator[:rim].astype(jnp.bfloat16), "row", -1).astype(jnp.float32),
    )
    from_prev = (
        shifted(numerator[-rim:].astype(jnp.bfloat16), "row", 1).astype(jnp.float32),
        shifted(denominator[-rim:].astype(jnp.bfloat16), "row", 1).astype(jnp.float32),
    )
    middle_num = numerator[rim:-rim]
    middle_den = denominator[rim:-rim]
    middle_num = middle_num.at[:rim].add(from_prev[0]).at[-rim:].add(from_next[0])
    middle_den = middle_den.at[:rim].add(from_prev[1]).at[-rim:].add(from_next[1])
    return (middle_num, middle_den)


def fold_cols(numerator, denominator, rim):
    from_next = (
        shifted(numerator[:, :rim].astype(jnp.bfloat16), "col", -1).astype(jnp.float32),
        shifted(denominator[:, :rim].astype(jnp.bfloat16), "col", -1).astype(jnp.float32),
    )
    from_prev = (
        shifted(numerator[:, -rim:].astype(jnp.bfloat16), "col", 1).astype(jnp.float32),
        shifted(denominator[:, -rim:].astype(jnp.bfloat16), "col", 1).astype(jnp.float32),
    )
    middle_num = numerator[:, rim:-rim] + jnp.concatenate([from_prev[0], from_next[0]], axis=1)
    middle_den = denominator[:, rim:-rim] + jnp.concatenate([from_prev[1], from_next[1]], axis=1)
    return (middle_num, middle_den)


def body(embeddings, pos_embed, ln_gain, ln_bias, w_qkv, b_qkv, w_out, b_out, valid):
    tile = embeddings.shape[1]
    tile_rows = embeddings.shape[0] // tile
    rim = tile // 2
    win = tile + 2 * rim
    rows_count = win * win
    width_model = embeddings.shape[2]
    window = extended(embeddings, (("row", 0), ("col", 1)), rim)
    stacked = jnp.stack([window], axis=0)
    inputs = stacked.reshape(tile_rows, rows_count, width_model).astype(
        jnp.float32
    ) + pos_embed.astype(jnp.float32)
    inputs = inputs.reshape(tile_rows * rows_count, width_model)
    normed = layer_norm(inputs, ln_gain, ln_bias).astype(jnp.bfloat16)
    projected = jnp.dot(
        normed,
        lax.all_gather(w_qkv, ("row", "col"), axis=0, tiled=True),
        preferred_element_type=jnp.float32,
    )
    projected = (
        (projected + b_qkv).astype(jnp.bfloat16).reshape(tile_rows, rows_count, w_qkv.shape[1])
    )
    attended = jax.vmap(attend)(projected).reshape(tile_rows * rows_count, -1)
    projected_out = lax.dot_general(
        attended,
        lax.all_gather(w_out, ("row", "col"), axis=0, tiled=True),
        (((1,), (1,)), ((), ())),
        preferred_element_type=jnp.float32,
    )
    hidden = inputs + projected_out + b_out
    gauss = gauss_table(win).reshape(1, rows_count)
    weight = gauss * valid.reshape(tile_rows, rows_count).astype(jnp.float32) / 196.0
    contrib = (weight.reshape(tile_rows * rows_count, 1) * hidden).reshape(
        tile_rows, win, win, width_model
    )
    weight_grid = weight.reshape(tile_rows, win, win)
    numerator = jnp.zeros((tile_rows * tile + 2 * rim, win, width_model), jnp.float32)
    denominator = jnp.zeros((tile_rows * tile + 2 * rim, win), jnp.float32)
    numerator = numerator.at[0:win].add(contrib[0])
    denominator = denominator.at[0:win].add(weight_grid[0])
    numerator, denominator = fold_rows(numerator, denominator, rim)
    numerator, denominator = fold_cols(numerator, denominator, rim)
    return (numerator / jnp.maximum(denominator, FLOOR)[:, :, None]).astype(jnp.bfloat16)


def solution(mesh):
    placed = (
        P(("groups", "row"), "col", None),
        P(),
        P(),
        P(),
        P(("row", "col"), None),
        P(),
        P(("row", "col"), None),
        P(),
        P(("groups", "row"), "col", None),
    )
    rows = mesh.shape["row"]

    def run(*arrays):
        embeddings, w_qkv = arrays[0], arrays[4]
        tile = embeddings.shape[1]
        whole_tiles = w_qkv.shape[0] % 16 == 0 and embeddings.shape[0] == tile == 8
        pairs = mesh.shape["groups"] == 2 and mesh.shape["col"] == 2
        if whole_tiles and pairs and rows == 8:
            return fused(rows, *arrays)
        return body(*arrays)

    return jax.shard_map(
        run,
        mesh=mesh,
        in_specs=placed,
        out_specs=P(("groups", "row"), "col", None),
        check_vma=False,
    )
```

```python
import functools

import jax
import jax.numpy as jnp
from jax import lax
from jax.experimental import pallas as pl
from jax.experimental.pallas import tpu as pltpu
from jax.sharding import PartitionSpec as P

HEADS = 8
EPSILON = 1e-06
SPREAD = 4.0
FLOOR = 0.25
LANES = 128
MESH = pl.DeviceIdType.MESH


def kernel(
    rows,
    emb_ref, pos_hbm, gain_hbm, bias_hbm, wq_ref, bq_hbm, wo_ref, bo_hbm, valid_ref,
    out_ref, pos_ref, gain_ref, bias_ref, bq_ref, bo_ref,
    eb, vb, wq_all, wo_all, nrm, proj, posr, base, wcol, att, near_out, near_in,
    far_out, far_in, send_sems, recv_sems, local_sems,
):
    g, r, c = lax.axis_index("groups"), lax.axis_index("row"), lax.axis_index("col")
    half = rows // 2
    tile, _, width = emb_ref.shape
    rim = tile // 2
    win = 2 * tile
    tok = win * win
    shard = wq_ref.shape[0]
    qkv = wq_ref.shape[1]
    hd = wo_ref.shape[1]
    head = hd // HEADS
    p = jnp.where(r % 2 == 0, r // 2, rows - 1 - r // 2)

    def row_at(position):
        q = lax.rem(position + 2 * rows, rows)
        return jnp.where(q < half, 2 * q, 2 * (rows - 1 - q) + 1)

    d = 1 - 2 * c
    ahead, behind = row_at(p + d), row_at(p - d)
    above, below = lax.rem(r + rows - 1, rows), lax.rem(r + 1, rows)
    other = 1 - c
    to_core, to_y = (g, r, other), (1 - g, r, c)

    names = {}

    def copy(name, src, dst, device):
        at = names.setdefault(name, len(names))
        return pltpu.make_async_remote_copy(
            src_ref=src, dst_ref=dst, send_sem=send_sems.at[at], recv_sem=recv_sems.at[at],
            device_id=device, device_id_type=MESH,
        )

    pending = []

    def start(name, src, dst, device):
        item = copy(name, src, dst, device)
        item.start()
        pending.append(item)

    def arrived(name, dst):
        copy(name, dst, dst, to_core).wait_recv()

    own_rows = pl.ds(tile // 2, tile)
    locals_ = []
    for src, dst in (
        (emb_ref, eb.at[0, own_rows]), (valid_ref, vb.at[1]), (pos_hbm, pos_ref),
        (gain_hbm, gain_ref), (bias_hbm, bias_ref), (bo_hbm, bo_ref), (bq_hbm, bq_ref),
        (wq_ref, wq_all.at[r, c]), (wo_ref, wo_all.at[r, c]),
    ):
        item = pltpu.make_async_copy(src, dst, local_sems.at[len(locals_)])
        item.start()
        locals_.append(item)

    barrier = pltpu.get_barrier_semaphore()
    has_above, has_below = r > 0, r < rows - 1
    for peer in (to_core, to_y, (g, ahead, c), (g, behind, c)):
        pl.semaphore_signal(barrier, inc=1, device_id=peer, device_id_type=MESH)

    @pl.when(has_above)
    def _():
        for core in (c, other):
            pl.semaphore_signal(barrier, inc=1, device_id=(g, above, core), device_id_type=MESH)

    @pl.when(has_below)
    def _():
        for core in (c, other):
            pl.semaphore_signal(barrier, inc=1, device_id=(g, below, core), device_id_type=MESH)

    pl.semaphore_wait(barrier, 8 - 2 * (r == 0).astype(jnp.int32) - 2 * (r == rows - 1).astype(jnp.int32))

    halo_down = copy("hd", emb_ref.at[pl.ds(tile - rim, rim)], eb.at[0, pl.ds(0, rim)], (g, below, c))
    halo_up = copy("hu", emb_ref.at[pl.ds(0, rim)], eb.at[0, pl.ds(rim + tile, rim)], (g, above, c))

    count_down = [copy("v0", valid_ref, vb.at[0], (g, below, c)), copy("v3", valid_ref, vb.at[3], (g, below, other))]
    count_up = [copy("v2", valid_ref, vb.at[2], (g, above, c)), copy("v5", valid_ref, vb.at[5], (g, above, other))]

    @pl.when(has_below)
    def _():
        halo_down.start()
        for item in count_down:
            item.start()

    @pl.when(has_above)
    def _():
        halo_up.start()
        for item in count_up:
            item.start()

    start("ec", emb_ref, eb.at[1, own_rows], to_core)
    start("v4", valid_ref, vb.at[4], to_core)

    class Stream:
        def __init__(self, name, ref, gathered, first, units):
            self.name, self.ref, self.all = name, ref, gathered
            side = (units + 1) // 3
            self.cols = pl.ds(first * LANES, units * LANES)
            self.ring_w, self.y_w = (units - side) * LANES, side * LANES
            self.ring = pl.ds(pl.multiple_of(first * LANES + g * self.y_w, LANES), self.ring_w)
            self.y_out = pl.ds(pl.multiple_of(first * LANES + g * self.ring_w, LANES), self.y_w)
            self.y_in = pl.ds(pl.multiple_of(first * LANES + (1 - g) * self.ring_w, LANES), self.y_w)

        def shard_row(self, way, step):
            return row_at(p - d * (step + 1)) if way == 0 else row_at(p + d * (step + 1))

        def place(self, row, core, cols):
            return self.all.at[row, core, :, cols]

        def send(self, way, step):
            row = r if step == 0 else self.shard_row(way, step - 1)
            src = self.ref.at[:, self.ring] if step == 0 else self.place(row, c, self.ring)
            device = (g, ahead if way == 0 else behind, c)
            start(f"{self.name}r{way}{step}", src, self.place(row, c, self.ring), device)

        def begin(self):
            self.send(0, 0)
            self.send(1, 0)

        def own(self):
            start(f"{self.name}o", self.ref.at[:, self.cols], self.place(r, c, self.cols), to_core)

        def ways(self, step):
            return (0, 1) if step < half - 1 else (0,)

        def ring_recv(self, step):
            for way in self.ways(step):
                row = self.shard_row(way, step)
                here = self.place(row, c, self.ring)
                arrived(f"{self.name}r{way}{step}", here)
                if way in self.ways(step + 1) and step + 1 < half:
                    self.send(way, step + 1)
                if step < half - 1:
                    side = self.place(row, c, self.y_out)
                    start(f"{self.name}y{way}{step}", side, side, to_y)
                start(f"{self.name}c{way}{step}", here, here, to_core)

        def y_recv(self, step):
            for way in self.ways(step):
                row = self.shard_row(way, step)
                here = self.place(row, c, self.y_in)
                if step < half - 1:
                    arrived(f"{self.name}y{way}{step}", here)
                    if step == half - 2 and way == 0:
                        start(f"{self.name}l", here, here, (g, ahead, c))
                else:
                    arrived(f"{self.name}l", here)
                start(f"{self.name}d{way}{step}", here, here, to_core)

        def core_recv(self, step):
            for way in self.ways(step):
                row = row_at(p + d * (step + 1)) if way == 0 else row_at(p - d * (step + 1))
                arrived(f"{self.name}c{way}{step}", self.place(row, other, self.ring))
                arrived(f"{self.name}d{way}{step}", self.place(row, other, self.y_in))

        def own_recv(self):
            arrived(f"{self.name}o", self.place(r, other, self.cols))

    units = qkv // LANES
    early = (units + 1) // 2
    parts = [Stream("q", wq_ref, wq_all, 0, early), Stream("k", wq_ref, wq_all, early, units - early)]
    ws = Stream("w", wo_ref, wo_all, 0, hd // LANES)
    for part in parts:
        part.begin()
    for part in parts:
        part.own()
    ws.own()

    @pl.when(r == 0)
    def _():
        eb[0, 0:rim] = jnp.zeros((rim, tile, width), eb.dtype)
        eb[1, 0:rim] = jnp.zeros((rim, tile, width), eb.dtype)
        vb[0] = jnp.zeros((1, 1, tok), vb.dtype)
        vb[3] = jnp.zeros((1, 1, tok), vb.dtype)

    @pl.when(r == rows - 1)
    def _():
        eb[0, rim + tile:] = jnp.zeros((rim, tile, width), eb.dtype)
        eb[1, rim + tile:] = jnp.zeros((rim, tile, width), eb.dtype)
        vb[2] = jnp.zeros((1, 1, tok), vb.dtype)
        vb[5] = jnp.zeros((1, 1, tok), vb.dtype)

    arrived("ec", eb.at[1, own_rows])
    fwd_top = copy("ft", eb.at[0, pl.ds(0, rim)], eb.at[1, pl.ds(0, rim)], to_core)
    fwd_bot = copy("fb", eb.at[0, pl.ds(rim + tile, rim)], eb.at[1, pl.ds(rim + tile, rim)], to_core)

    @pl.when(r > 0)
    def _():
        halo_down.wait_recv()
        fwd_top.start()

    @pl.when(r < rows - 1)
    def _():
        halo_up.wait_recv()
        fwd_bot.start()

    @pl.when(r > 0)
    def _():
        fwd_top.wait_recv()

    @pl.when(r < rows - 1)
    def _():
        fwd_bot.wait_recv()

    parts[0].ring_recv(0)

    for item in locals_[:6]:
        item.wait()
    gain, bias = gain_ref[...].reshape(1, width), bias_ref[...].reshape(1, width)
    span = 2 * shard
    per = rim
    place = lax.broadcasted_iota(jnp.int32, (per, tile, 1), 1)
    rim_ok = jnp.where(c == 0, place, tile - 1 - place) < rim

    def norm_block(block, carry):
        at = pl.ds(block * per, per)
        left = eb[0, at].astype(jnp.float32)
        right = jnp.where(rim_ok, eb[1, at].astype(jnp.float32), 0.0)
        pos = pos_ref[pl.ds(pl.multiple_of(block * per * win, per * win), per * win)]
        pos = pos.astype(jnp.float32).reshape(per, win, width)
        pos = pltpu.roll(pos, win - rim, 1)
        posr[at] = pos
        x = (jnp.concatenate([left, right], axis=1) + pos).reshape(per * win, width)
        x = x - jnp.mean(x, axis=-1, keepdims=True)
        variance = jnp.mean(x * x, axis=-1, keepdims=True)
        x = x * lax.rsqrt(variance + EPSILON) * gain + bias
        there = pl.ds(pl.multiple_of(block * per * win, per * win), per * win)
        for k in range(rows):
            nrm[k, there] = x[:, k * span:(k + 1) * span].astype(jnp.bfloat16)
        return carry

    lax.fori_loop(0, win // per, norm_block, 0)

    parts[1].ring_recv(0)
    ws.begin()

    arrived("v4", vb.at[4])

    @pl.when(has_above)
    def _():
        for item in count_down:
            item.wait_recv()

    @pl.when(has_below)
    def _():
        for item in count_up:
            item.wait_recv()

    counts = [vb[0, 0], vb[1, 0], vb[2, 0], vb[3, 0], vb[4, 0], vb[5, 0]]
    counts = jnp.concatenate(
        [v.astype(jnp.float32) for v in counts] + [jnp.zeros((2, tok), jnp.float32)], axis=0
    ).astype(jnp.bfloat16)
    t_row = lax.broadcasted_iota(jnp.int32, (tok, tok), 0)
    t_col = lax.broadcasted_iota(jnp.int32, (tok, tok), 1)
    base_row = t_row // win * win
    pick = (t_col == base_row + (t_row - base_row + rim) % win).astype(jnp.float32).astype(jnp.bfloat16)
    counts = lax.dot_general(pick, counts, (((1,), (1,)), ((), ())), preferred_element_type=jnp.float32)
    t = lax.broadcasted_iota(jnp.int32, (tok, 1), 0)
    oi = (t // win).astype(jnp.float32) - (win - 1) / 2.0
    oj = ((t % win + rim) % win).astype(jnp.float32) - (win - 1) / 2.0
    gauss = jnp.exp(-(oi * oi + oj * oj) / (2.0 * SPREAD * SPREAD))
    weights = gauss * counts / 196.0
    wcol[...] = weights
    grid = weights.reshape(win, win, 8)
    near = grid[:, :tile].reshape(win * tile, 8)
    far = grid[:, tile:].reshape(win * tile, 8)
    u = lax.broadcasted_iota(jnp.int32, (win * tile, 1), 0) % tile
    fold_ok = jnp.where(c == 1, u, tile - 1 - u) < rim
    far = jnp.where(fold_ok, far, 0.0)
    low, high = rim * tile, (rim + tile) * tile
    near0, far0 = near[low:high, 1:2], far[low:high, 4:5]
    near_a = jnp.where(has_above, near[high:, 0:1], 0.0)
    far_a = jnp.where(has_above, far[high:, 3:4], 0.0)
    near_b = jnp.where(has_below, near[:low, 2:3], 0.0)
    far_b = jnp.where(has_below, far[:low, 5:6], 0.0)
    denom = near0 + far0 + jnp.concatenate([near_a + far_a, near_b + far_b], axis=0)

    def flat(lo, hi, a, b):
        return posr[lo:hi, a:b].reshape((hi - lo) * (b - a), width)

    total = denom * (
        eb[0, rim:rim + tile].astype(jnp.float32).reshape(tile * tile, width)
        + bo_ref[...].reshape(1, width)
    )
    total += near0 * flat(rim, rim + tile, 0, tile) + far0 * flat(rim, rim + tile, tile, win)
    base[...] = total
    base[0:low] += near_a * flat(rim + tile, win, 0, tile) + far_a * flat(rim + tile, win, tile, win)
    base[low:] += near_b * flat(0, rim, 0, tile) + far_b * flat(0, rim, tile, win)

    block_n = qkv // 3

    def multiply(row, first=False):
        def part(n, carry):
            cols = pl.ds(pl.multiple_of(n * block_n, LANES), block_n)
            got = jnp.dot(
                nrm[row], wq_all[row, :, :, cols].reshape(span, block_n),
                preferred_element_type=jnp.float32,
            )
            if first:
                proj[:, cols] = got + bq_ref[cols].reshape(1, block_n)
            else:
                proj[:, cols] += got
            return carry

        lax.fori_loop(0, 3, part, 0)

    for item in locals_[6:]:
        item.wait()
    for part in parts:
        part.own_recv()
    multiply(r, True)

    for step in range(1, half):
        last = step == half - 1
        if not last:
            for part in parts:
                part.ring_recv(step)
        for part in parts:
            part.y_recv(step - 1)
        for part in parts:
            part.core_recv(step - 1)
        multiply(row_at(p - step))
        multiply(row_at(p + step))
        if last:
            for part in parts:
                part.ring_recv(step)
        ws.ring_recv(step - 1)
        if step >= 2:
            ws.y_recv(step - 2)
    for part in parts:
        part.y_recv(half - 1)
    for part in parts:
        part.core_recv(half - 1)
    multiply(row_at(p + half))

    def attend(h):
        lo, hi = h * head, (h + 1) * head
        a, b = lo // LANES * LANES, -(-hi // LANES) * LANES
        lane = lax.broadcasted_iota(jnp.int32, (1, b - a), 1) + a
        inside = (lane >= lo) & (lane < hi)
        q = jnp.where(inside, proj[:, a:b], 0.0).astype(jnp.bfloat16)
        k = proj[:, hd + a:hd + b].astype(jnp.bfloat16)
        v = proj[:, 2 * hd + a:2 * hd + b].astype(jnp.bfloat16)
        scores = lax.dot_general(
            q, k, (((1,), (1,)), ((), ())), preferred_element_type=jnp.float32
        ) * head ** (-0.5)
        expon = jnp.exp(scores - jnp.max(scores, axis=-1, keepdims=True))
        probs = (expon / jnp.sum(expon, axis=-1, keepdims=True)).astype(jnp.bfloat16)
        mixed = jnp.dot(probs, v, preferred_element_type=jnp.float32)
        att[:, a:b] = mixed if lo == a else jnp.where(inside, mixed, att[:, a:b])

    for h in range(HEADS // 2):
        attend(h)
    ws.y_recv(half - 2)
    for h in range(HEADS // 2, HEADS):
        attend(h)
    ws.ring_recv(half - 1)

    merged = att[...].astype(jnp.bfloat16).astype(jnp.float32) * wcol[:, 1:2]
    merged = merged.reshape(win, win, hd)
    near_out[...] = merged[:, :tile].reshape(win * tile, hd).astype(jnp.bfloat16)
    far_out[...] = merged[:, tile:].reshape(win * tile, hd).astype(jnp.bfloat16)
    top, mid, bottom = pl.ds(0, low), pl.ds(low, high - low), pl.ds(high, low)
    send_up = [copy("rt", near_out.at[top], near_in.at[bottom], (g, above, c)),
               copy("st", far_out.at[top], far_in.at[bottom], (g, above, other))]
    send_down = [copy("rb", near_out.at[bottom], near_in.at[top], (g, below, c)),
                 copy("sb", far_out.at[bottom], far_in.at[top], (g, below, other))]

    @pl.when(has_above)
    def _():
        for item in send_up:
            item.start()

    @pl.when(has_below)
    def _():
        for item in send_down:
            item.start()

    start("rc", far_out.at[mid], far_in.at[mid], to_core)
    own = merged[:, :tile].reshape(win * tile, hd)[low:high]

    @pl.when(r == 0)
    def _():
        near_in[0:low] = jnp.zeros((low, hd), near_in.dtype)
        far_in[0:low] = jnp.zeros((low, hd), far_in.dtype)

    @pl.when(r == rows - 1)
    def _():
        near_in[high:] = jnp.zeros((low, hd), near_in.dtype)
        far_in[high:] = jnp.zeros((low, hd), far_in.dtype)

    ws.y_recv(half - 1)
    for step in range(half):
        ws.core_recv(step)
    ws.own_recv()
    arrived("rc", far_in.at[mid])

    @pl.when(has_above)
    def _():
        for item in send_down:
            item.wait_recv()

    @pl.when(has_below)
    def _():
        for item in send_up:
            item.wait_recv()

    far_got = jnp.where(fold_ok, far_in[...].astype(jnp.float32), 0.0)
    edge = jnp.concatenate(
        [near_in[0:low].astype(jnp.float32) + far_got[:low],
         near_in[high:].astype(jnp.float32) + far_got[high:]], axis=0
    )
    own = own + far_got[low:high] + edge
    result = base[...] + lax.dot_general(
        own.astype(jnp.bfloat16), wo_all[...].reshape(width, hd),
        (((1,), (1,)), ((), ())), preferred_element_type=jnp.float32,
    )
    result = result / jnp.maximum(denom, FLOOR)
    out_ref[...] = result.reshape(tile, tile, width).astype(out_ref.dtype)

    for item in pending:
        item.wait_send()

    @pl.when(has_above)
    def _():
        for item in [halo_up, fwd_top] + count_up + send_up:
            item.wait_send()

    @pl.when(has_below)
    def _():
        for item in [halo_down, fwd_bot] + count_down + send_down:
            item.wait_send()


def fused(rows, embeddings, pos_embed, ln_gain, ln_bias, w_qkv, b_qkv, w_out, b_out, valid):
    tile, _, width = embeddings.shape
    win, rim = 2 * tile, tile // 2
    tok = win * win
    shard, qkv = w_qkv.shape
    hd = w_out.shape[1]
    bf16, f32 = jnp.bfloat16, jnp.float32
    vmem = pl.BlockSpec(memory_space=pltpu.VMEM)
    return pl.pallas_call(
        functools.partial(kernel, rows),
        out_shape=jax.ShapeDtypeStruct(embeddings.shape, bf16),
        in_specs=[pl.BlockSpec(memory_space=pltpu.HBM)] * 9,
        out_specs=vmem,
        scratch_shapes=[
            pltpu.VMEM((tok, width), bf16),
            pltpu.VMEM((width,), f32),
            pltpu.VMEM((width,), f32),
            pltpu.VMEM((qkv,), f32),
            pltpu.VMEM((width,), f32),
            pltpu.VMEM((2, win, tile, width), bf16),
            pltpu.VMEM((6, 1, 1, tok), jnp.int32),
            pltpu.VMEM((rows, 2, shard, qkv), bf16),
            pltpu.VMEM((rows, 2, shard, hd), bf16),
            pltpu.VMEM((rows, tok, 2 * shard), bf16),
            pltpu.VMEM((tok, qkv), f32),
            pltpu.VMEM((win, win, width), f32),
            pltpu.VMEM((tile * tile, width), f32),
            pltpu.VMEM((tok, 8), f32),
            pltpu.VMEM((tok, hd), f32),
            pltpu.VMEM((win * tile, hd), bf16),
            pltpu.VMEM((win * tile, hd), bf16),
            pltpu.VMEM((win * tile, hd), bf16),
            pltpu.VMEM((win * tile, hd), bf16),
            pltpu.SemaphoreType.DMA((16 + 20 * rows,)),
            pltpu.SemaphoreType.DMA((16 + 20 * rows,)),
            pltpu.SemaphoreType.DMA((9,)),
        ],
        compiler_params=pltpu.CompilerParams(
            collective_id=0, has_side_effects=True, vmem_limit_bytes=67043328
        ),
    )(
        embeddings, pos_embed, ln_gain, ln_bias, w_qkv, b_qkv, w_out, b_out, valid
    )


def shifted(value, axis, steps):
    count = lax.axis_size(axis)
    initial, last = (max(0, -steps), min(count, count - steps))
    return lax.ppermute(value, axis, [(source, source + steps) for source in range(initial, last)])


def extended(block, sides, width):
    for axis, dim in sides:
        count = lax.axis_size(axis)
        forward = [(i, i + 1) for i in range(count - 1)]
        backward = [(target, source) for source, target in forward]
        low = lax.ppermute(
            lax.slice_in_dim(block, block.shape[dim] - width, None, axis=dim), axis, forward
        )
        high = lax.ppermute(lax.slice_in_dim(block, 0, width, axis=dim), axis, backward)
        block = jnp.concatenate([low, block, high], axis=dim)
    return block


def layer_norm(inputs, ln_gain, ln_bias):
    centred = inputs - jnp.mean(inputs, axis=-1, keepdims=True)
    variance = jnp.mean(centred * centred, axis=-1, keepdims=True)
    return centred * lax.rsqrt(variance + EPSILON) * ln_gain + ln_bias


def gauss_table(win):
    offsets = jnp.arange(win, dtype=jnp.float32) - (win - 1) / 2.0
    squared = offsets[:, None] * offsets[:, None] + offsets[None, :] * offsets[None, :]
    return jnp.exp(-squared / (2.0 * SPREAD * SPREAD))


def attend(projected):
    rows_count = projected.shape[0]
    width = projected.shape[1] // 3
    head_size = width // HEADS
    queries = projected[:, :width].reshape(rows_count, HEADS, head_size)
    keys = projected[:, width : 2 * width].reshape(rows_count, HEADS, head_size)
    values = projected[:, 2 * width :].reshape(rows_count, HEADS, head_size)
    scores = jnp.einsum(
        "qhd,khd->hqk", queries, keys, preferred_element_type=jnp.float32
    ) * head_size ** (-0.5)
    highest = jnp.max(scores, axis=-1, keepdims=True)
    expon = jnp.exp(scores - highest)
    probs = (expon / jnp.sum(expon, axis=-1, keepdims=True)).astype(jnp.bfloat16)
    mixed = jnp.einsum("hqk,khd->qhd", probs, values, preferred_element_type=jnp.float32)
    return mixed.astype(jnp.bfloat16).reshape(rows_count, width)


def fold_rows(numerator, denominator, rim):
    from_next = (
        shifted(numerator[:rim].astype(jnp.bfloat16), "row", -1).astype(jnp.float32),
        shifted(denominator[:rim].astype(jnp.bfloat16), "row", -1).astype(jnp.float32),
    )
    from_prev = (
        shifted(numerator[-rim:].astype(jnp.bfloat16), "row", 1).astype(jnp.float32),
        shifted(denominator[-rim:].astype(jnp.bfloat16), "row", 1).astype(jnp.float32),
    )
    middle_num = numerator[rim:-rim]
    middle_den = denominator[rim:-rim]
    middle_num = middle_num.at[:rim].add(from_prev[0]).at[-rim:].add(from_next[0])
    middle_den = middle_den.at[:rim].add(from_prev[1]).at[-rim:].add(from_next[1])
    return (middle_num, middle_den)


def fold_cols(numerator, denominator, rim):
    from_next = (
        shifted(numerator[:, :rim].astype(jnp.bfloat16), "col", -1).astype(jnp.float32),
        shifted(denominator[:, :rim].astype(jnp.bfloat16), "col", -1).astype(jnp.float32),
    )
    from_prev = (
        shifted(numerator[:, -rim:].astype(jnp.bfloat16), "col", 1).astype(jnp.float32),
        shifted(denominator[:, -rim:].astype(jnp.bfloat16), "col", 1).astype(jnp.float32),
    )
    middle_num = numerator[:, rim:-rim] + jnp.concatenate([from_prev[0], from_next[0]], axis=1)
    middle_den = denominator[:, rim:-rim] + jnp.concatenate([from_prev[1], from_next[1]], axis=1)
    return (middle_num, middle_den)


def body(embeddings, pos_embed, ln_gain, ln_bias, w_qkv, b_qkv, w_out, b_out, valid):
    tile = embeddings.shape[1]
    tile_rows = embeddings.shape[0] // tile
    rim = tile // 2
    win = tile + 2 * rim
    rows_count = win * win
    width_model = embeddings.shape[2]
    window = extended(embeddings, (("row", 0), ("col", 1)), rim)
    stacked = jnp.stack([window], axis=0)
    inputs = stacked.reshape(tile_rows, rows_count, width_model).astype(
        jnp.float32
    ) + pos_embed.astype(jnp.float32)
    inputs = inputs.reshape(tile_rows * rows_count, width_model)
    normed = layer_norm(inputs, ln_gain, ln_bias).astype(jnp.bfloat16)
    projected = jnp.dot(
        normed,
        lax.all_gather(w_qkv, ("row", "col"), axis=0, tiled=True),
        preferred_element_type=jnp.float32,
    )
    projected = (
        (projected + b_qkv).astype(jnp.bfloat16).reshape(tile_rows, rows_count, w_qkv.shape[1])
    )
    attended = jax.vmap(attend)(projected).reshape(tile_rows * rows_count, -1)
    projected_out = lax.dot_general(
        attended,
        lax.all_gather(w_out, ("row", "col"), axis=0, tiled=True),
        (((1,), (1,)), ((), ())),
        preferred_element_type=jnp.float32,
    )
    hidden = inputs + projected_out + b_out
    gauss = gauss_table(win).reshape(1, rows_count)
    weight = gauss * valid.reshape(tile_rows, rows_count).astype(jnp.float32) / 196.0
    contrib = (weight.reshape(tile_rows * rows_count, 1) * hidden).reshape(
        tile_rows, win, win, width_model
    )
    weight_grid = weight.reshape(tile_rows, win, win)
    numerator = jnp.zeros((tile_rows * tile + 2 * rim, win, width_model), jnp.float32)
    denominator = jnp.zeros((tile_rows * tile + 2 * rim, win), jnp.float32)
    numerator = numerator.at[0:win].add(contrib[0])
    denominator = denominator.at[0:win].add(weight_grid[0])
    numerator, denominator = fold_rows(numerator, denominator, rim)
    numerator, denominator = fold_cols(numerator, denominator, rim)
    return (numerator / jnp.maximum(denominator, FLOOR)[:, :, None]).astype(jnp.bfloat16)


def solution(mesh):
    placed = (
        P(("groups", "row"), "col", None),
        P(),
        P(),
        P(),
        P(("row", "col"), None),
        P(),
        P(("row", "col"), None),
        P(),
        P(("groups", "row"), "col", None),
    )
    rows = mesh.shape["row"]

    def run(*arrays):
        embeddings, w_qkv = arrays[0], arrays[4]
        tile = embeddings.shape[1]
        whole_tiles = w_qkv.shape[0] % 16 == 0 and embeddings.shape[0] == tile == 8
        pairs = mesh.shape["groups"] == 2 and mesh.shape["col"] == 2
        if whole_tiles and pairs and rows == 8:
            return fused(rows, *arrays)
        return body(*arrays)

    return jax.shard_map(
        run,
        mesh=mesh,
        in_specs=placed,
        out_specs=P(("groups", "row"), "col", None),
        check_vma=False,
    )
```

```python
import functools

import jax
import jax.numpy as jnp
from jax import lax
from jax.experimental import pallas as pl
from jax.experimental.pallas import tpu as pltpu
from jax.sharding import PartitionSpec as P

HEADS = 8
EPSILON = 1e-06
SPREAD = 4.0
FLOOR = 0.25
LANES = 128
MESH = pl.DeviceIdType.MESH


def kernel(
    rows,
    emb_ref, pos_hbm, gain_hbm, bias_hbm, wq_ref, bq_hbm, wo_ref, bo_hbm, valid_ref,
    out_ref, pos_ref, gain_ref, bias_ref, bq_ref, bo_ref,
    eb, vb, wq_all, wo_all, nrm, proj, posr, base, wcol, att, near_out, near_in,
    far_out, far_in, send_sems, recv_sems, local_sems,
):
    g, r, c = lax.axis_index("groups"), lax.axis_index("row"), lax.axis_index("col")
    half = rows // 2
    tile, _, width = emb_ref.shape
    rim = tile // 2
    win = 2 * tile
    tok = win * win
    shard = wq_ref.shape[0]
    qkv = wq_ref.shape[1]
    hd = wo_ref.shape[1]
    head = hd // HEADS
    p = jnp.where(r % 2 == 0, r // 2, rows - 1 - r // 2)

    def row_at(position):
        q = lax.rem(position + 2 * rows, rows)
        return jnp.where(q < half, 2 * q, 2 * (rows - 1 - q) + 1)

    d = 1 - 2 * c
    ahead, behind = row_at(p + d), row_at(p - d)
    above, below = lax.rem(r + rows - 1, rows), lax.rem(r + 1, rows)
    other = 1 - c
    to_core, to_y = (g, r, other), (1 - g, r, c)

    names = {}

    def copy(name, src, dst, device):
        at = names.setdefault(name, len(names))
        return pltpu.make_async_remote_copy(
            src_ref=src, dst_ref=dst, send_sem=send_sems.at[at], recv_sem=recv_sems.at[at],
            device_id=device, device_id_type=MESH,
        )

    pending = []

    def start(name, src, dst, device):
        item = copy(name, src, dst, device)
        item.start()
        pending.append(item)

    def arrived(name, dst):
        copy(name, dst, dst, to_core).wait_recv()

    own_rows = pl.ds(tile // 2, tile)
    locals_ = []
    for src, dst in (
        (emb_ref, eb.at[0, own_rows]), (valid_ref, vb.at[1]), (pos_hbm, pos_ref),
        (gain_hbm, gain_ref), (bias_hbm, bias_ref), (bo_hbm, bo_ref), (bq_hbm, bq_ref),
        (wq_ref, wq_all.at[r, c]), (wo_ref, wo_all.at[r, c]),
    ):
        item = pltpu.make_async_copy(src, dst, local_sems.at[len(locals_)])
        item.start()
        locals_.append(item)

    barrier = pltpu.get_barrier_semaphore()
    has_above, has_below = r > 0, r < rows - 1
    for peer in (to_core, to_y, (g, ahead, c), (g, behind, c)):
        pl.semaphore_signal(barrier, inc=1, device_id=peer, device_id_type=MESH)

    @pl.when(has_above)
    def _():
        for core in (c, other):
            pl.semaphore_signal(barrier, inc=1, device_id=(g, above, core), device_id_type=MESH)

    @pl.when(has_below)
    def _():
        for core in (c, other):
            pl.semaphore_signal(barrier, inc=1, device_id=(g, below, core), device_id_type=MESH)

    pl.semaphore_wait(barrier, 8 - 2 * (r == 0).astype(jnp.int32) - 2 * (r == rows - 1).astype(jnp.int32))

    halo_down = copy("hd", emb_ref.at[pl.ds(tile - rim, rim)], eb.at[0, pl.ds(0, rim)], (g, below, c))
    halo_up = copy("hu", emb_ref.at[pl.ds(0, rim)], eb.at[0, pl.ds(rim + tile, rim)], (g, above, c))

    count_down = [copy("v0", valid_ref, vb.at[0], (g, below, c)), copy("v3", valid_ref, vb.at[3], (g, below, other))]
    count_up = [copy("v2", valid_ref, vb.at[2], (g, above, c)), copy("v5", valid_ref, vb.at[5], (g, above, other))]

    @pl.when(has_below)
    def _():
        halo_down.start()
        for item in count_down:
            item.start()

    @pl.when(has_above)
    def _():
        halo_up.start()
        for item in count_up:
            item.start()

    start("ec", emb_ref, eb.at[1, own_rows], to_core)
    start("v4", valid_ref, vb.at[4], to_core)

    class Stream:
        def __init__(self, name, ref, gathered, first, units):
            self.name, self.ref, self.all = name, ref, gathered
            side = (units + 1) // 3
            self.cols = pl.ds(first * LANES, units * LANES)
            self.ring_w, self.y_w = (units - side) * LANES, side * LANES
            self.ring = pl.ds(pl.multiple_of(first * LANES + g * self.y_w, LANES), self.ring_w)
            self.y_out = pl.ds(pl.multiple_of(first * LANES + g * self.ring_w, LANES), self.y_w)
            self.y_in = pl.ds(pl.multiple_of(first * LANES + (1 - g) * self.ring_w, LANES), self.y_w)

        def shard_row(self, way, step):
            return row_at(p - d * (step + 1)) if way == 0 else row_at(p + d * (step + 1))

        def place(self, row, core, cols):
            return self.all.at[row, core, :, cols]

        def send(self, way, step):
            row = r if step == 0 else self.shard_row(way, step - 1)
            src = self.ref.at[:, self.ring] if step == 0 else self.place(row, c, self.ring)
            device = (g, ahead if way == 0 else behind, c)
            start(f"{self.name}r{way}{step}", src, self.place(row, c, self.ring), device)

        def begin(self):
            self.send(0, 0)
            self.send(1, 0)

        def own(self):
            start(f"{self.name}o", self.ref.at[:, self.cols], self.place(r, c, self.cols), to_core)

        def ways(self, step):
            return (0, 1) if step < half - 1 else (0,)

        def ring_recv(self, step):
            for way in self.ways(step):
                row = self.shard_row(way, step)
                here = self.place(row, c, self.ring)
                arrived(f"{self.name}r{way}{step}", here)
                if way in self.ways(step + 1) and step + 1 < half:
                    self.send(way, step + 1)
                if step < half - 1:
                    side = self.place(row, c, self.y_out)
                    start(f"{self.name}y{way}{step}", side, side, to_y)
                start(f"{self.name}c{way}{step}", here, here, to_core)

        def y_recv(self, step):
            for way in self.ways(step):
                row = self.shard_row(way, step)
                here = self.place(row, c, self.y_in)
                if step < half - 1:
                    arrived(f"{self.name}y{way}{step}", here)
                    if step == half - 2 and way == 0:
                        start(f"{self.name}l", here, here, (g, ahead, c))
                else:
                    arrived(f"{self.name}l", here)
                start(f"{self.name}d{way}{step}", here, here, to_core)

        def core_recv(self, step):
            for way in self.ways(step):
                row = row_at(p + d * (step + 1)) if way == 0 else row_at(p - d * (step + 1))
                arrived(f"{self.name}c{way}{step}", self.place(row, other, self.ring))
                arrived(f"{self.name}d{way}{step}", self.place(row, other, self.y_in))

        def own_recv(self):
            arrived(f"{self.name}o", self.place(r, other, self.cols))

    units = qkv // LANES
    early = (units + 1) // 2
    parts = [Stream("q", wq_ref, wq_all, 0, early), Stream("k", wq_ref, wq_all, early, units - early)]
    ws = Stream("w", wo_ref, wo_all, 0, hd // LANES)
    for part in parts:
        part.begin()
    for part in parts:
        part.own()
    ws.own()

    @pl.when(r == 0)
    def _():
        eb[0, 0:rim] = jnp.zeros((rim, tile, width), eb.dtype)
        eb[1, 0:rim] = jnp.zeros((rim, tile, width), eb.dtype)
        vb[0] = jnp.zeros((1, 1, tok), vb.dtype)
        vb[3] = jnp.zeros((1, 1, tok), vb.dtype)

    @pl.when(r == rows - 1)
    def _():
        eb[0, rim + tile:] = jnp.zeros((rim, tile, width), eb.dtype)
        eb[1, rim + tile:] = jnp.zeros((rim, tile, width), eb.dtype)
        vb[2] = jnp.zeros((1, 1, tok), vb.dtype)
        vb[5] = jnp.zeros((1, 1, tok), vb.dtype)

    arrived("ec", eb.at[1, own_rows])
    fwd_top = copy("ft", eb.at[0, pl.ds(0, rim)], eb.at[1, pl.ds(0, rim)], to_core)
    fwd_bot = copy("fb", eb.at[0, pl.ds(rim + tile, rim)], eb.at[1, pl.ds(rim + tile, rim)], to_core)

    @pl.when(r > 0)
    def _():
        halo_down.wait_recv()
        fwd_top.start()

    @pl.when(r < rows - 1)
    def _():
        halo_up.wait_recv()
        fwd_bot.start()

    @pl.when(r > 0)
    def _():
        fwd_top.wait_recv()

    @pl.when(r < rows - 1)
    def _():
        fwd_bot.wait_recv()

    parts[0].ring_recv(0)

    for item in locals_[:6]:
        item.wait()
    gain, bias = gain_ref[...].reshape(1, width), bias_ref[...].reshape(1, width)
    span = 2 * shard
    per = rim
    place = lax.broadcasted_iota(jnp.int32, (per, tile, 1), 1)
    rim_ok = jnp.where(c == 0, place, tile - 1 - place) < rim

    def norm_block(block, carry):
        at = pl.ds(block * per, per)
        left = eb[0, at].astype(jnp.float32)
        right = jnp.where(rim_ok, eb[1, at].astype(jnp.float32), 0.0)
        pos = pos_ref[pl.ds(pl.multiple_of(block * per * win, per * win), per * win)]
        pos = pos.astype(jnp.float32).reshape(per, win, width)
        pos = pltpu.roll(pos, win - rim, 1)
        posr[at] = pos
        x = (jnp.concatenate([left, right], axis=1) + pos).reshape(per * win, width)
        x = x - jnp.mean(x, axis=-1, keepdims=True)
        variance = jnp.mean(x * x, axis=-1, keepdims=True)
        x = x * lax.rsqrt(variance + EPSILON) * gain + bias
        there = pl.ds(pl.multiple_of(block * per * win, per * win), per * win)
        for k in range(rows):
            nrm[k, there] = x[:, k * span:(k + 1) * span].astype(jnp.bfloat16)
        return carry

    lax.fori_loop(0, win // per, norm_block, 0)

    parts[1].ring_recv(0)
    ws.begin()

    arrived("v4", vb.at[4])

    @pl.when(has_above)
    def _():
        for item in count_down:
            item.wait_recv()

    @pl.when(has_below)
    def _():
        for item in count_up:
            item.wait_recv()

    counts = [vb[0, 0], vb[1, 0], vb[2, 0], vb[3, 0], vb[4, 0], vb[5, 0]]
    counts = jnp.concatenate(
        [v.astype(jnp.float32) for v in counts] + [jnp.zeros((2, tok), jnp.float32)], axis=0
    ).astype(jnp.bfloat16)
    t_row = lax.broadcasted_iota(jnp.int32, (tok, tok), 0)
    t_col = lax.broadcasted_iota(jnp.int32, (tok, tok), 1)
    base_row = t_row // win * win
    pick = (t_col == base_row + (t_row - base_row + rim) % win).astype(jnp.float32).astype(jnp.bfloat16)
    counts = lax.dot_general(pick, counts, (((1,), (1,)), ((), ())), preferred_element_type=jnp.float32)
    t = lax.broadcasted_iota(jnp.int32, (tok, 1), 0)
    oi = (t // win).astype(jnp.float32) - (win - 1) / 2.0
    oj = ((t % win + rim) % win).astype(jnp.float32) - (win - 1) / 2.0
    gauss = jnp.exp(-(oi * oi + oj * oj) / (2.0 * SPREAD * SPREAD))
    weights = gauss * counts / 196.0
    wcol[...] = weights
    grid = weights.reshape(win, win, 8)
    near = grid[:, :tile].reshape(win * tile, 8)
    far = grid[:, tile:].reshape(win * tile, 8)
    u = lax.broadcasted_iota(jnp.int32, (win * tile, 1), 0) % tile
    fold_ok = jnp.where(c == 1, u, tile - 1 - u) < rim
    far = jnp.where(fold_ok, far, 0.0)
    low, high = rim * tile, (rim + tile) * tile
    near0, far0 = near[low:high, 1:2], far[low:high, 4:5]
    near_a = jnp.where(has_above, near[high:, 0:1], 0.0)
    far_a = jnp.where(has_above, far[high:, 3:4], 0.0)
    near_b = jnp.where(has_below, near[:low, 2:3], 0.0)
    far_b = jnp.where(has_below, far[:low, 5:6], 0.0)
    denom = near0 + far0 + jnp.concatenate([near_a + far_a, near_b + far_b], axis=0)

    def flat(lo, hi, a, b):
        return posr[lo:hi, a:b].reshape((hi - lo) * (b - a), width)

    total = denom * (
        eb[0, rim:rim + tile].astype(jnp.float32).reshape(tile * tile, width)
        + bo_ref[...].reshape(1, width)
    )
    total += near0 * flat(rim, rim + tile, 0, tile) + far0 * flat(rim, rim + tile, tile, win)
    base[...] = total
    base[0:low] += near_a * flat(rim + tile, win, 0, tile) + far_a * flat(rim + tile, win, tile, win)
    base[low:] += near_b * flat(0, rim, 0, tile) + far_b * flat(0, rim, tile, win)

    block_n = qkv // 3

    def multiply(row, first=False):
        def part(n, carry):
            cols = pl.ds(pl.multiple_of(n * block_n, LANES), block_n)
            got = jnp.dot(
                nrm[row], wq_all[row, :, :, cols].reshape(span, block_n),
                preferred_element_type=jnp.float32,
            )
            if first:
                proj[:, cols] = got + bq_ref[cols].reshape(1, block_n)
            else:
                proj[:, cols] += got
            return carry

        lax.fori_loop(0, 3, part, 0)

    for item in locals_[6:]:
        item.wait()
    for part in parts:
        part.own_recv()
    multiply(r, True)

    early_part, late_part = parts
    for step in range(1, half - 1):
        early_part.ring_recv(step)
        if step > 1:
            multiply(row_at(p + step - 1))
        late_part.ring_recv(step)
        for part in parts:
            part.y_recv(step - 1)
        ws.ring_recv(step - 1)
        for part in parts:
            part.core_recv(step - 1)
        multiply(row_at(p - step))
        if step >= 2:
            ws.y_recv(step - 2)
    for part in parts:
        part.y_recv(half - 2)
    multiply(row_at(p + half - 2))
    ws.ring_recv(half - 2)
    ws.y_recv(half - 3)
    for part in parts:
        part.ring_recv(half - 1)
    for part in parts:
        part.core_recv(half - 2)
    multiply(row_at(p - half + 1))
    multiply(row_at(p + half - 1))
    ws.y_recv(half - 2)
    for part in parts:
        part.y_recv(half - 1)
    for part in parts:
        part.core_recv(half - 1)
    multiply(row_at(p + half))

    def attend(h):
        lo, hi = h * head, (h + 1) * head
        a, b = lo // LANES * LANES, -(-hi // LANES) * LANES
        lane = lax.broadcasted_iota(jnp.int32, (1, b - a), 1) + a
        inside = (lane >= lo) & (lane < hi)
        q = jnp.where(inside, proj[:, a:b], 0.0).astype(jnp.bfloat16)
        k = proj[:, hd + a:hd + b].astype(jnp.bfloat16)
        v = proj[:, 2 * hd + a:2 * hd + b].astype(jnp.bfloat16)
        scores = lax.dot_general(
            q, k, (((1,), (1,)), ((), ())), preferred_element_type=jnp.float32
        ) * head ** (-0.5)
        expon = jnp.exp(scores - jnp.max(scores, axis=-1, keepdims=True))
        probs = (expon / jnp.sum(expon, axis=-1, keepdims=True)).astype(jnp.bfloat16)
        mixed = jnp.dot(probs, v, preferred_element_type=jnp.float32)
        att[:, a:b] = mixed if lo == a else jnp.where(inside, mixed, att[:, a:b])

    for h in range(HEADS // 2):
        attend(h)
    ws.ring_recv(half - 1)
    for h in range(HEADS // 2, HEADS):
        attend(h)

    merged = att[...].astype(jnp.bfloat16).astype(jnp.float32) * wcol[:, 1:2]
    merged = merged.reshape(win, win, hd)
    near_out[...] = merged[:, :tile].reshape(win * tile, hd).astype(jnp.bfloat16)
    far_out[...] = merged[:, tile:].reshape(win * tile, hd).astype(jnp.bfloat16)
    top, mid, bottom = pl.ds(0, low), pl.ds(low, high - low), pl.ds(high, low)
    send_up = [copy("rt", near_out.at[top], near_in.at[bottom], (g, above, c)),
               copy("st", far_out.at[top], far_in.at[bottom], (g, above, other))]
    send_down = [copy("rb", near_out.at[bottom], near_in.at[top], (g, below, c)),
                 copy("sb", far_out.at[bottom], far_in.at[top], (g, below, other))]

    @pl.when(has_above)
    def _():
        for item in send_up:
            item.start()

    @pl.when(has_below)
    def _():
        for item in send_down:
            item.start()

    start("rc", far_out.at[mid], far_in.at[mid], to_core)
    own = merged[:, :tile].reshape(win * tile, hd)[low:high]

    @pl.when(r == 0)
    def _():
        near_in[0:low] = jnp.zeros((low, hd), near_in.dtype)
        far_in[0:low] = jnp.zeros((low, hd), far_in.dtype)

    @pl.when(r == rows - 1)
    def _():
        near_in[high:] = jnp.zeros((low, hd), near_in.dtype)
        far_in[high:] = jnp.zeros((low, hd), far_in.dtype)

    ws.y_recv(half - 1)
    for step in range(half):
        ws.core_recv(step)
    ws.own_recv()
    arrived("rc", far_in.at[mid])

    @pl.when(has_above)
    def _():
        for item in send_down:
            item.wait_recv()

    @pl.when(has_below)
    def _():
        for item in send_up:
            item.wait_recv()

    far_got = jnp.where(fold_ok, far_in[...].astype(jnp.float32), 0.0)
    edge = jnp.concatenate(
        [near_in[0:low].astype(jnp.float32) + far_got[:low],
         near_in[high:].astype(jnp.float32) + far_got[high:]], axis=0
    )
    own = own + far_got[low:high] + edge
    result = base[...] + lax.dot_general(
        own.astype(jnp.bfloat16), wo_all[...].reshape(width, hd),
        (((1,), (1,)), ((), ())), preferred_element_type=jnp.float32,
    )
    result = result / jnp.maximum(denom, FLOOR)
    out_ref[...] = result.reshape(tile, tile, width).astype(out_ref.dtype)

    for item in pending:
        item.wait_send()

    @pl.when(has_above)
    def _():
        for item in [halo_up, fwd_top] + count_up + send_up:
            item.wait_send()

    @pl.when(has_below)
    def _():
        for item in [halo_down, fwd_bot] + count_down + send_down:
            item.wait_send()


def fused(rows, embeddings, pos_embed, ln_gain, ln_bias, w_qkv, b_qkv, w_out, b_out, valid):
    tile, _, width = embeddings.shape
    win, rim = 2 * tile, tile // 2
    tok = win * win
    shard, qkv = w_qkv.shape
    hd = w_out.shape[1]
    bf16, f32 = jnp.bfloat16, jnp.float32
    vmem = pl.BlockSpec(memory_space=pltpu.VMEM)
    return pl.pallas_call(
        functools.partial(kernel, rows),
        out_shape=jax.ShapeDtypeStruct(embeddings.shape, bf16),
        in_specs=[pl.BlockSpec(memory_space=pltpu.HBM)] * 9,
        out_specs=vmem,
        scratch_shapes=[
            pltpu.VMEM((tok, width), bf16),
            pltpu.VMEM((width,), f32),
            pltpu.VMEM((width,), f32),
            pltpu.VMEM((qkv,), f32),
            pltpu.VMEM((width,), f32),
            pltpu.VMEM((2, win, tile, width), bf16),
            pltpu.VMEM((6, 1, 1, tok), jnp.int32),
            pltpu.VMEM((rows, 2, shard, qkv), bf16),
            pltpu.VMEM((rows, 2, shard, hd), bf16),
            pltpu.VMEM((rows, tok, 2 * shard), bf16),
            pltpu.VMEM((tok, qkv), f32),
            pltpu.VMEM((win, win, width), f32),
            pltpu.VMEM((tile * tile, width), f32),
            pltpu.VMEM((tok, 8), f32),
            pltpu.VMEM((tok, hd), f32),
            pltpu.VMEM((win * tile, hd), bf16),
            pltpu.VMEM((win * tile, hd), bf16),
            pltpu.VMEM((win * tile, hd), bf16),
            pltpu.VMEM((win * tile, hd), bf16),
            pltpu.SemaphoreType.DMA((16 + 20 * rows,)),
            pltpu.SemaphoreType.DMA((16 + 20 * rows,)),
            pltpu.SemaphoreType.DMA((9,)),
        ],
        compiler_params=pltpu.CompilerParams(
            collective_id=0, has_side_effects=True, vmem_limit_bytes=67043328
        ),
    )(
        embeddings, pos_embed, ln_gain, ln_bias, w_qkv, b_qkv, w_out, b_out, valid
    )


def shifted(value, axis, steps):
    count = lax.axis_size(axis)
    initial, last = (max(0, -steps), min(count, count - steps))
    return lax.ppermute(value, axis, [(source, source + steps) for source in range(initial, last)])


def extended(block, sides, width):
    for axis, dim in sides:
        count = lax.axis_size(axis)
        forward = [(i, i + 1) for i in range(count - 1)]
        backward = [(target, source) for source, target in forward]
        low = lax.ppermute(
            lax.slice_in_dim(block, block.shape[dim] - width, None, axis=dim), axis, forward
        )
        high = lax.ppermute(lax.slice_in_dim(block, 0, width, axis=dim), axis, backward)
        block = jnp.concatenate([low, block, high], axis=dim)
    return block


def layer_norm(inputs, ln_gain, ln_bias):
    centred = inputs - jnp.mean(inputs, axis=-1, keepdims=True)
    variance = jnp.mean(centred * centred, axis=-1, keepdims=True)
    return centred * lax.rsqrt(variance + EPSILON) * ln_gain + ln_bias


def gauss_table(win):
    offsets = jnp.arange(win, dtype=jnp.float32) - (win - 1) / 2.0
    squared = offsets[:, None] * offsets[:, None] + offsets[None, :] * offsets[None, :]
    return jnp.exp(-squared / (2.0 * SPREAD * SPREAD))


def attend(projected):
    rows_count = projected.shape[0]
    width = projected.shape[1] // 3
    head_size = width // HEADS
    queries = projected[:, :width].reshape(rows_count, HEADS, head_size)
    keys = projected[:, width : 2 * width].reshape(rows_count, HEADS, head_size)
    values = projected[:, 2 * width :].reshape(rows_count, HEADS, head_size)
    scores = jnp.einsum(
        "qhd,khd->hqk", queries, keys, preferred_element_type=jnp.float32
    ) * head_size ** (-0.5)
    highest = jnp.max(scores, axis=-1, keepdims=True)
    expon = jnp.exp(scores - highest)
    probs = (expon / jnp.sum(expon, axis=-1, keepdims=True)).astype(jnp.bfloat16)
    mixed = jnp.einsum("hqk,khd->qhd", probs, values, preferred_element_type=jnp.float32)
    return mixed.astype(jnp.bfloat16).reshape(rows_count, width)


def fold_rows(numerator, denominator, rim):
    from_next = (
        shifted(numerator[:rim].astype(jnp.bfloat16), "row", -1).astype(jnp.float32),
        shifted(denominator[:rim].astype(jnp.bfloat16), "row", -1).astype(jnp.float32),
    )
    from_prev = (
        shifted(numerator[-rim:].astype(jnp.bfloat16), "row", 1).astype(jnp.float32),
        shifted(denominator[-rim:].astype(jnp.bfloat16), "row", 1).astype(jnp.float32),
    )
    middle_num = numerator[rim:-rim]
    middle_den = denominator[rim:-rim]
    middle_num = middle_num.at[:rim].add(from_prev[0]).at[-rim:].add(from_next[0])
    middle_den = middle_den.at[:rim].add(from_prev[1]).at[-rim:].add(from_next[1])
    return (middle_num, middle_den)


def fold_cols(numerator, denominator, rim):
    from_next = (
        shifted(numerator[:, :rim].astype(jnp.bfloat16), "col", -1).astype(jnp.float32),
        shifted(denominator[:, :rim].astype(jnp.bfloat16), "col", -1).astype(jnp.float32),
    )
    from_prev = (
        shifted(numerator[:, -rim:].astype(jnp.bfloat16), "col", 1).astype(jnp.float32),
        shifted(denominator[:, -rim:].astype(jnp.bfloat16), "col", 1).astype(jnp.float32),
    )
    middle_num = numerator[:, rim:-rim] + jnp.concatenate([from_prev[0], from_next[0]], axis=1)
    middle_den = denominator[:, rim:-rim] + jnp.concatenate([from_prev[1], from_next[1]], axis=1)
    return (middle_num, middle_den)


def body(embeddings, pos_embed, ln_gain, ln_bias, w_qkv, b_qkv, w_out, b_out, valid):
    tile = embeddings.shape[1]
    tile_rows = embeddings.shape[0] // tile
    rim = tile // 2
    win = tile + 2 * rim
    rows_count = win * win
    width_model = embeddings.shape[2]
    window = extended(embeddings, (("row", 0), ("col", 1)), rim)
    stacked = jnp.stack([window], axis=0)
    inputs = stacked.reshape(tile_rows, rows_count, width_model).astype(
        jnp.float32
    ) + pos_embed.astype(jnp.float32)
    inputs = inputs.reshape(tile_rows * rows_count, width_model)
    normed = layer_norm(inputs, ln_gain, ln_bias).astype(jnp.bfloat16)
    projected = jnp.dot(
        normed,
        lax.all_gather(w_qkv, ("row", "col"), axis=0, tiled=True),
        preferred_element_type=jnp.float32,
    )
    projected = (
        (projected + b_qkv).astype(jnp.bfloat16).reshape(tile_rows, rows_count, w_qkv.shape[1])
    )
    attended = jax.vmap(attend)(projected).reshape(tile_rows * rows_count, -1)
    projected_out = lax.dot_general(
        attended,
        lax.all_gather(w_out, ("row", "col"), axis=0, tiled=True),
        (((1,), (1,)), ((), ())),
        preferred_element_type=jnp.float32,
    )
    hidden = inputs + projected_out + b_out
    gauss = gauss_table(win).reshape(1, rows_count)
    weight = gauss * valid.reshape(tile_rows, rows_count).astype(jnp.float32) / 196.0
    contrib = (weight.reshape(tile_rows * rows_count, 1) * hidden).reshape(
        tile_rows, win, win, width_model
    )
    weight_grid = weight.reshape(tile_rows, win, win)
    numerator = jnp.zeros((tile_rows * tile + 2 * rim, win, width_model), jnp.float32)
    denominator = jnp.zeros((tile_rows * tile + 2 * rim, win), jnp.float32)
    numerator = numerator.at[0:win].add(contrib[0])
    denominator = denominator.at[0:win].add(weight_grid[0])
    numerator, denominator = fold_rows(numerator, denominator, rim)
    numerator, denominator = fold_cols(numerator, denominator, rim)
    return (numerator / jnp.maximum(denominator, FLOOR)[:, :, None]).astype(jnp.bfloat16)


def solution(mesh):
    placed = (
        P(("groups", "row"), "col", None),
        P(),
        P(),
        P(),
        P(("row", "col"), None),
        P(),
        P(("row", "col"), None),
        P(),
        P(("groups", "row"), "col", None),
    )
    rows = mesh.shape["row"]

    def run(*arrays):
        embeddings, w_qkv = arrays[0], arrays[4]
        tile = embeddings.shape[1]
        whole_tiles = w_qkv.shape[0] % 16 == 0 and embeddings.shape[0] == tile == 8
        pairs = mesh.shape["groups"] == 2 and mesh.shape["col"] == 2
        if whole_tiles and pairs and rows == 8:
            return fused(rows, *arrays)
        return body(*arrays)

    return jax.shard_map(
        run,
        mesh=mesh,
        in_specs=placed,
        out_specs=P(("groups", "row"), "col", None),
        check_vma=False,
    )
```

```python
import functools

import jax
import jax.numpy as jnp
from jax import lax
from jax.experimental import pallas as pl
from jax.experimental.pallas import tpu as pltpu
from jax.sharding import PartitionSpec as P

HEADS = 8
EPSILON = 1e-06
SPREAD = 4.0
FLOOR = 0.25
LANES = 128
MESH = pl.DeviceIdType.MESH


def kernel(
    rows,
    emb_ref, pos_hbm, gain_hbm, bias_hbm, wq_ref, bq_hbm, wo_ref, bo_hbm, valid_ref,
    out_ref, pos_ref, gain_ref, bias_ref, bq_ref, bo_ref,
    eb, vb, wq_all, wo_all, nrm, proj, posr, base, wcol, att, near_out, near_in,
    far_out, far_in, send_sems, recv_sems, local_sems,
):
    g, r, c = lax.axis_index("groups"), lax.axis_index("row"), lax.axis_index("col")
    half = rows // 2
    tile, _, width = emb_ref.shape
    rim = tile // 2
    win = 2 * tile
    tok = win * win
    shard = wq_ref.shape[0]
    qkv = wq_ref.shape[1]
    hd = wo_ref.shape[1]
    head = hd // HEADS
    p = jnp.where(r % 2 == 0, r // 2, rows - 1 - r // 2)

    def row_at(position):
        q = lax.rem(position + 2 * rows, rows)
        return jnp.where(q < half, 2 * q, 2 * (rows - 1 - q) + 1)

    d = 1 - 2 * c
    ahead, behind = row_at(p + d), row_at(p - d)
    above, below = lax.rem(r + rows - 1, rows), lax.rem(r + 1, rows)
    other = 1 - c
    to_core, to_y = (g, r, other), (1 - g, r, c)

    names = {}

    def copy(name, src, dst, device):
        at = names.setdefault(name, len(names))
        return pltpu.make_async_remote_copy(
            src_ref=src, dst_ref=dst, send_sem=send_sems.at[at], recv_sem=recv_sems.at[at],
            device_id=device, device_id_type=MESH,
        )

    pending = []

    def start(name, src, dst, device):
        item = copy(name, src, dst, device)
        item.start()
        pending.append(item)

    def arrived(name, dst):
        copy(name, dst, dst, to_core).wait_recv()

    own_rows = pl.ds(tile // 2, tile)
    locals_ = []
    for src, dst in (
        (emb_ref, eb.at[0, own_rows]), (valid_ref, vb.at[1]), (pos_hbm, pos_ref),
        (gain_hbm, gain_ref), (bias_hbm, bias_ref), (bo_hbm, bo_ref), (bq_hbm, bq_ref),
        (wq_ref, wq_all.at[r, c]), (wo_ref, wo_all.at[r, c]),
    ):
        item = pltpu.make_async_copy(src, dst, local_sems.at[len(locals_)])
        item.start()
        locals_.append(item)

    barrier = pltpu.get_barrier_semaphore()
    has_above, has_below = r > 0, r < rows - 1
    for peer in (to_core, to_y, (g, ahead, c), (g, behind, c), (g, ahead, other)):
        pl.semaphore_signal(barrier, inc=1, device_id=peer, device_id_type=MESH)

    @pl.when(has_above)
    def _():
        for core in (c, other):
            pl.semaphore_signal(barrier, inc=1, device_id=(g, above, core), device_id_type=MESH)

    @pl.when(has_below)
    def _():
        for core in (c, other):
            pl.semaphore_signal(barrier, inc=1, device_id=(g, below, core), device_id_type=MESH)

    pl.semaphore_wait(barrier, 9 - 2 * (r == 0).astype(jnp.int32) - 2 * (r == rows - 1).astype(jnp.int32))

    halo_down = copy("hd", emb_ref.at[pl.ds(tile - rim, rim)], eb.at[0, pl.ds(0, rim)], (g, below, c))
    halo_up = copy("hu", emb_ref.at[pl.ds(0, rim)], eb.at[0, pl.ds(rim + tile, rim)], (g, above, c))

    count_down = [copy("v0", valid_ref, vb.at[0], (g, below, c)), copy("v3", valid_ref, vb.at[3], (g, below, other))]
    count_up = [copy("v2", valid_ref, vb.at[2], (g, above, c)), copy("v5", valid_ref, vb.at[5], (g, above, other))]

    @pl.when(has_below)
    def _():
        halo_down.start()
        for item in count_down:
            item.start()

    @pl.when(has_above)
    def _():
        halo_up.start()
        for item in count_up:
            item.start()

    start("ec", emb_ref, eb.at[1, own_rows], to_core)
    start("v4", valid_ref, vb.at[4], to_core)

    class Stream:
        def __init__(self, name, ref, gathered, first, units):
            self.name, self.ref, self.all = name, ref, gathered
            side = (units + 1) // 3
            self.cols = pl.ds(first * LANES, units * LANES)
            self.ring_w, self.y_w = (units - side) * LANES, side * LANES
            self.ring = pl.ds(pl.multiple_of(first * LANES + g * self.y_w, LANES), self.ring_w)
            self.y_out = pl.ds(pl.multiple_of(first * LANES + g * self.ring_w, LANES), self.y_w)
            self.y_in = pl.ds(pl.multiple_of(first * LANES + (1 - g) * self.ring_w, LANES), self.y_w)

        def shard_row(self, way, step):
            return row_at(p - d * (step + 1)) if way == 0 else row_at(p + d * (step + 1))

        def place(self, row, core, cols):
            return self.all.at[row, core, :, cols]

        def send(self, way, step):
            row = r if step == 0 else self.shard_row(way, step - 1)
            src = self.ref.at[:, self.ring] if step == 0 else self.place(row, c, self.ring)
            device = (g, ahead if way == 0 else behind, c)
            start(f"{self.name}r{way}{step}", src, self.place(row, c, self.ring), device)

        def begin(self):
            self.send(0, 0)
            self.send(1, 0)

        def own(self):
            start(f"{self.name}o", self.ref.at[:, self.cols], self.place(r, c, self.cols), to_core)

        def ways(self, step):
            return (0, 1) if step < half - 1 else (0,)

        def ring_recv(self, step):
            for way in self.ways(step):
                row = self.shard_row(way, step)
                here = self.place(row, c, self.ring)
                arrived(f"{self.name}r{way}{step}", here)
                if way in self.ways(step + 1) and step + 1 < half:
                    self.send(way, step + 1)
                if step < half - 1:
                    side = self.place(row, c, self.y_out)
                    start(f"{self.name}y{way}{step}", side, side, to_y)
                start(f"{self.name}c{way}{step}", here, here, to_core)

        def y_recv(self, step):
            for way in self.ways(step):
                row = self.shard_row(way, step)
                here = self.place(row, c, self.y_in)
                if step < half - 1:
                    arrived(f"{self.name}y{way}{step}", here)
                    if step == half - 2 and way == 0:
                        start(f"{self.name}l", here, here, (g, ahead, c))
                        start(f"{self.name}d{way}{half - 1}", here, here, (g, ahead, other))
                else:
                    arrived(f"{self.name}l", here)
                if step < half - 1:
                    start(f"{self.name}d{way}{step}", here, here, to_core)

        def core_recv(self, step):
            for way in self.ways(step):
                row = row_at(p + d * (step + 1)) if way == 0 else row_at(p - d * (step + 1))
                arrived(f"{self.name}c{way}{step}", self.place(row, other, self.ring))
                arrived(f"{self.name}d{way}{step}", self.place(row, other, self.y_in))

        def own_recv(self):
            arrived(f"{self.name}o", self.place(r, other, self.cols))

    units = qkv // LANES
    early = (units + 1) // 2
    parts = [Stream("q", wq_ref, wq_all, 0, early), Stream("k", wq_ref, wq_all, early, units - early)]
    ws = Stream("w", wo_ref, wo_all, 0, hd // LANES)
    for part in parts:
        part.begin()
    for part in parts:
        part.own()
    ws.own()

    @pl.when(r == 0)
    def _():
        eb[0, 0:rim] = jnp.zeros((rim, tile, width), eb.dtype)
        eb[1, 0:rim] = jnp.zeros((rim, tile, width), eb.dtype)
        vb[0] = jnp.zeros((1, 1, tok), vb.dtype)
        vb[3] = jnp.zeros((1, 1, tok), vb.dtype)

    @pl.when(r == rows - 1)
    def _():
        eb[0, rim + tile:] = jnp.zeros((rim, tile, width), eb.dtype)
        eb[1, rim + tile:] = jnp.zeros((rim, tile, width), eb.dtype)
        vb[2] = jnp.zeros((1, 1, tok), vb.dtype)
        vb[5] = jnp.zeros((1, 1, tok), vb.dtype)

    arrived("ec", eb.at[1, own_rows])
    fwd_top = copy("ft", eb.at[0, pl.ds(0, rim)], eb.at[1, pl.ds(0, rim)], to_core)
    fwd_bot = copy("fb", eb.at[0, pl.ds(rim + tile, rim)], eb.at[1, pl.ds(rim + tile, rim)], to_core)

    @pl.when(r > 0)
    def _():
        halo_down.wait_recv()
        fwd_top.start()

    @pl.when(r < rows - 1)
    def _():
        halo_up.wait_recv()
        fwd_bot.start()

    @pl.when(r > 0)
    def _():
        fwd_top.wait_recv()

    @pl.when(r < rows - 1)
    def _():
        fwd_bot.wait_recv()

    parts[0].ring_recv(0)

    for item in locals_[:6]:
        item.wait()
    gain, bias = gain_ref[...].reshape(1, width), bias_ref[...].reshape(1, width)
    span = 2 * shard
    per = rim
    place = lax.broadcasted_iota(jnp.int32, (per, tile, 1), 1)
    rim_ok = jnp.where(c == 0, place, tile - 1 - place) < rim

    def norm_block(block, carry):
        at = pl.ds(block * per, per)
        left = eb[0, at].astype(jnp.float32)
        right = jnp.where(rim_ok, eb[1, at].astype(jnp.float32), 0.0)
        pos = pos_ref[pl.ds(pl.multiple_of(block * per * win, per * win), per * win)]
        pos = pos.astype(jnp.float32).reshape(per, win, width)
        pos = pltpu.roll(pos, win - rim, 1)
        posr[at] = pos
        x = (jnp.concatenate([left, right], axis=1) + pos).reshape(per * win, width)
        x = x - jnp.mean(x, axis=-1, keepdims=True)
        variance = jnp.mean(x * x, axis=-1, keepdims=True)
        x = x * lax.rsqrt(variance + EPSILON) * gain + bias
        there = pl.ds(pl.multiple_of(block * per * win, per * win), per * win)
        for k in range(rows):
            nrm[k, there] = x[:, k * span:(k + 1) * span].astype(jnp.bfloat16)
        return carry

    lax.fori_loop(0, win // per, norm_block, 0)

    parts[1].ring_recv(0)
    ws.begin()

    arrived("v4", vb.at[4])

    @pl.when(has_above)
    def _():
        for item in count_down:
            item.wait_recv()

    @pl.when(has_below)
    def _():
        for item in count_up:
            item.wait_recv()

    counts = [vb[0, 0], vb[1, 0], vb[2, 0], vb[3, 0], vb[4, 0], vb[5, 0]]
    counts = jnp.concatenate(
        [v.astype(jnp.float32) for v in counts] + [jnp.zeros((2, tok), jnp.float32)], axis=0
    ).astype(jnp.bfloat16)
    t_row = lax.broadcasted_iota(jnp.int32, (tok, tok), 0)
    t_col = lax.broadcasted_iota(jnp.int32, (tok, tok), 1)
    base_row = t_row // win * win
    pick = (t_col == base_row + (t_row - base_row + rim) % win).astype(jnp.float32).astype(jnp.bfloat16)
    counts = lax.dot_general(pick, counts, (((1,), (1,)), ((), ())), preferred_element_type=jnp.float32)
    t = lax.broadcasted_iota(jnp.int32, (tok, 1), 0)
    oi = (t // win).astype(jnp.float32) - (win - 1) / 2.0
    oj = ((t % win + rim) % win).astype(jnp.float32) - (win - 1) / 2.0
    gauss = jnp.exp(-(oi * oi + oj * oj) / (2.0 * SPREAD * SPREAD))
    weights = gauss * counts / 196.0
    wcol[...] = weights
    grid = weights.reshape(win, win, 8)
    near = grid[:, :tile].reshape(win * tile, 8)
    far = grid[:, tile:].reshape(win * tile, 8)
    u = lax.broadcasted_iota(jnp.int32, (win * tile, 1), 0) % tile
    fold_ok = jnp.where(c == 1, u, tile - 1 - u) < rim
    far = jnp.where(fold_ok, far, 0.0)
    low, high = rim * tile, (rim + tile) * tile
    near0, far0 = near[low:high, 1:2], far[low:high, 4:5]
    near_a = jnp.where(has_above, near[high:, 0:1], 0.0)
    far_a = jnp.where(has_above, far[high:, 3:4], 0.0)
    near_b = jnp.where(has_below, near[:low, 2:3], 0.0)
    far_b = jnp.where(has_below, far[:low, 5:6], 0.0)
    denom = near0 + far0 + jnp.concatenate([near_a + far_a, near_b + far_b], axis=0)

    def flat(lo, hi, a, b):
        return posr[lo:hi, a:b].reshape((hi - lo) * (b - a), width)

    total = denom * (
        eb[0, rim:rim + tile].astype(jnp.float32).reshape(tile * tile, width)
        + bo_ref[...].reshape(1, width)
    )
    total += near0 * flat(rim, rim + tile, 0, tile) + far0 * flat(rim, rim + tile, tile, win)
    base[...] = total
    base[0:low] += near_a * flat(rim + tile, win, 0, tile) + far_a * flat(rim + tile, win, tile, win)
    base[low:] += near_b * flat(0, rim, 0, tile) + far_b * flat(0, rim, tile, win)

    block_n = qkv // 3

    def multiply(row, first=False):
        def part(n, carry):
            cols = pl.ds(pl.multiple_of(n * block_n, LANES), block_n)
            got = jnp.dot(
                nrm[row], wq_all[row, :, :, cols].reshape(span, block_n),
                preferred_element_type=jnp.float32,
            )
            if first:
                proj[:, cols] = got + bq_ref[cols].reshape(1, block_n)
            else:
                proj[:, cols] += got
            return carry

        lax.fori_loop(0, 3, part, 0)

    for item in locals_[6:]:
        item.wait()
    for part in parts:
        part.own_recv()
    multiply(r, True)

    early_part, late_part = parts
    for step in range(1, half - 1):
        early_part.ring_recv(step)
        if step > 1:
            multiply(row_at(p + step - 1))
        late_part.ring_recv(step)
        for part in parts:
            part.y_recv(step - 1)
        ws.ring_recv(step - 1)
        for part in parts:
            part.core_recv(step - 1)
        multiply(row_at(p - step))
        if step >= 2:
            ws.y_recv(step - 2)
    for part in parts:
        part.y_recv(half - 2)
    multiply(row_at(p + half - 2))
    ws.ring_recv(half - 2)
    ws.y_recv(half - 3)
    for part in parts:
        part.ring_recv(half - 1)
    for part in parts:
        part.core_recv(half - 2)
    multiply(row_at(p - half + 1))
    multiply(row_at(p + half - 1))
    ws.y_recv(half - 2)
    for part in parts:
        part.y_recv(half - 1)
    for part in parts:
        part.core_recv(half - 1)
    multiply(row_at(p + half))

    def attend(h):
        lo, hi = h * head, (h + 1) * head
        a, b = lo // LANES * LANES, -(-hi // LANES) * LANES
        lane = lax.broadcasted_iota(jnp.int32, (1, b - a), 1) + a
        inside = (lane >= lo) & (lane < hi)
        q = jnp.where(inside, proj[:, a:b], 0.0).astype(jnp.bfloat16)
        k = proj[:, hd + a:hd + b].astype(jnp.bfloat16)
        v = proj[:, 2 * hd + a:2 * hd + b].astype(jnp.bfloat16)
        scores = lax.dot_general(
            q, k, (((1,), (1,)), ((), ())), preferred_element_type=jnp.float32
        ) * head ** (-0.5)
        expon = jnp.exp(scores - jnp.max(scores, axis=-1, keepdims=True))
        probs = (expon / jnp.sum(expon, axis=-1, keepdims=True)).astype(jnp.bfloat16)
        mixed = jnp.dot(probs, v, preferred_element_type=jnp.float32)
        att[:, a:b] = mixed if lo == a else jnp.where(inside, mixed, att[:, a:b])

    for h in range(HEADS // 2):
        attend(h)
    ws.ring_recv(half - 1)
    for h in range(HEADS // 2, HEADS):
        attend(h)

    merged = att[...].astype(jnp.bfloat16).astype(jnp.float32) * wcol[:, 1:2]
    merged = merged.reshape(win, win, hd)
    near_out[...] = merged[:, :tile].reshape(win * tile, hd).astype(jnp.bfloat16)
    far_out[...] = merged[:, tile:].reshape(win * tile, hd).astype(jnp.bfloat16)
    top, mid, bottom = pl.ds(0, low), pl.ds(low, high - low), pl.ds(high, low)
    send_up = [copy("rt", near_out.at[top], near_in.at[bottom], (g, above, c)),
               copy("st", far_out.at[top], far_in.at[bottom], (g, above, other))]
    send_down = [copy("rb", near_out.at[bottom], near_in.at[top], (g, below, c)),
                 copy("sb", far_out.at[bottom], far_in.at[top], (g, below, other))]

    @pl.when(has_above)
    def _():
        for item in send_up:
            item.start()

    @pl.when(has_below)
    def _():
        for item in send_down:
            item.start()

    start("rc", far_out.at[mid], far_in.at[mid], to_core)
    own = merged[:, :tile].reshape(win * tile, hd)[low:high]

    @pl.when(r == 0)
    def _():
        near_in[0:low] = jnp.zeros((low, hd), near_in.dtype)
        far_in[0:low] = jnp.zeros((low, hd), far_in.dtype)

    @pl.when(r == rows - 1)
    def _():
        near_in[high:] = jnp.zeros((low, hd), near_in.dtype)
        far_in[high:] = jnp.zeros((low, hd), far_in.dtype)

    ws.y_recv(half - 1)
    for step in range(half):
        ws.core_recv(step)
    ws.own_recv()
    arrived("rc", far_in.at[mid])

    @pl.when(has_above)
    def _():
        for item in send_down:
            item.wait_recv()

    @pl.when(has_below)
    def _():
        for item in send_up:
            item.wait_recv()

    far_got = jnp.where(fold_ok, far_in[...].astype(jnp.float32), 0.0)
    edge = jnp.concatenate(
        [near_in[0:low].astype(jnp.float32) + far_got[:low],
         near_in[high:].astype(jnp.float32) + far_got[high:]], axis=0
    )
    own = own + far_got[low:high] + edge
    result = base[...] + lax.dot_general(
        own.astype(jnp.bfloat16), wo_all[...].reshape(width, hd),
        (((1,), (1,)), ((), ())), preferred_element_type=jnp.float32,
    )
    result = result / jnp.maximum(denom, FLOOR)
    out_ref[...] = result.reshape(tile, tile, width).astype(out_ref.dtype)

    for item in pending:
        item.wait_send()

    @pl.when(has_above)
    def _():
        for item in [halo_up, fwd_top] + count_up + send_up:
            item.wait_send()

    @pl.when(has_below)
    def _():
        for item in [halo_down, fwd_bot] + count_down + send_down:
            item.wait_send()


def fused(rows, embeddings, pos_embed, ln_gain, ln_bias, w_qkv, b_qkv, w_out, b_out, valid):
    tile, _, width = embeddings.shape
    win, rim = 2 * tile, tile // 2
    tok = win * win
    shard, qkv = w_qkv.shape
    hd = w_out.shape[1]
    bf16, f32 = jnp.bfloat16, jnp.float32
    vmem = pl.BlockSpec(memory_space=pltpu.VMEM)
    return pl.pallas_call(
        functools.partial(kernel, rows),
        out_shape=jax.ShapeDtypeStruct(embeddings.shape, bf16),
        in_specs=[pl.BlockSpec(memory_space=pltpu.HBM)] * 9,
        out_specs=vmem,
        scratch_shapes=[
            pltpu.VMEM((tok, width), bf16),
            pltpu.VMEM((width,), f32),
            pltpu.VMEM((width,), f32),
            pltpu.VMEM((qkv,), f32),
            pltpu.VMEM((width,), f32),
            pltpu.VMEM((2, win, tile, width), bf16),
            pltpu.VMEM((6, 1, 1, tok), jnp.int32),
            pltpu.VMEM((rows, 2, shard, qkv), bf16),
            pltpu.VMEM((rows, 2, shard, hd), bf16),
            pltpu.VMEM((rows, tok, 2 * shard), bf16),
            pltpu.VMEM((tok, qkv), f32),
            pltpu.VMEM((win, win, width), f32),
            pltpu.VMEM((tile * tile, width), f32),
            pltpu.VMEM((tok, 8), f32),
            pltpu.VMEM((tok, hd), f32),
            pltpu.VMEM((win * tile, hd), bf16),
            pltpu.VMEM((win * tile, hd), bf16),
            pltpu.VMEM((win * tile, hd), bf16),
            pltpu.VMEM((win * tile, hd), bf16),
            pltpu.SemaphoreType.DMA((16 + 20 * rows,)),
            pltpu.SemaphoreType.DMA((16 + 20 * rows,)),
            pltpu.SemaphoreType.DMA((9,)),
        ],
        compiler_params=pltpu.CompilerParams(
            collective_id=0, has_side_effects=True, vmem_limit_bytes=67043328
        ),
    )(
        embeddings, pos_embed, ln_gain, ln_bias, w_qkv, b_qkv, w_out, b_out, valid
    )


def shifted(value, axis, steps):
    count = lax.axis_size(axis)
    initial, last = (max(0, -steps), min(count, count - steps))
    return lax.ppermute(value, axis, [(source, source + steps) for source in range(initial, last)])


def extended(block, sides, width):
    for axis, dim in sides:
        count = lax.axis_size(axis)
        forward = [(i, i + 1) for i in range(count - 1)]
        backward = [(target, source) for source, target in forward]
        low = lax.ppermute(
            lax.slice_in_dim(block, block.shape[dim] - width, None, axis=dim), axis, forward
        )
        high = lax.ppermute(lax.slice_in_dim(block, 0, width, axis=dim), axis, backward)
        block = jnp.concatenate([low, block, high], axis=dim)
    return block


def layer_norm(inputs, ln_gain, ln_bias):
    centred = inputs - jnp.mean(inputs, axis=-1, keepdims=True)
    variance = jnp.mean(centred * centred, axis=-1, keepdims=True)
    return centred * lax.rsqrt(variance + EPSILON) * ln_gain + ln_bias


def gauss_table(win):
    offsets = jnp.arange(win, dtype=jnp.float32) - (win - 1) / 2.0
    squared = offsets[:, None] * offsets[:, None] + offsets[None, :] * offsets[None, :]
    return jnp.exp(-squared / (2.0 * SPREAD * SPREAD))


def attend(projected):
    rows_count = projected.shape[0]
    width = projected.shape[1] // 3
    head_size = width // HEADS
    queries = projected[:, :width].reshape(rows_count, HEADS, head_size)
    keys = projected[:, width : 2 * width].reshape(rows_count, HEADS, head_size)
    values = projected[:, 2 * width :].reshape(rows_count, HEADS, head_size)
    scores = jnp.einsum(
        "qhd,khd->hqk", queries, keys, preferred_element_type=jnp.float32
    ) * head_size ** (-0.5)
    highest = jnp.max(scores, axis=-1, keepdims=True)
    expon = jnp.exp(scores - highest)
    probs = (expon / jnp.sum(expon, axis=-1, keepdims=True)).astype(jnp.bfloat16)
    mixed = jnp.einsum("hqk,khd->qhd", probs, values, preferred_element_type=jnp.float32)
    return mixed.astype(jnp.bfloat16).reshape(rows_count, width)


def fold_rows(numerator, denominator, rim):
    from_next = (
        shifted(numerator[:rim].astype(jnp.bfloat16), "row", -1).astype(jnp.float32),
        shifted(denominator[:rim].astype(jnp.bfloat16), "row", -1).astype(jnp.float32),
    )
    from_prev = (
        shifted(numerator[-rim:].astype(jnp.bfloat16), "row", 1).astype(jnp.float32),
        shifted(denominator[-rim:].astype(jnp.bfloat16), "row", 1).astype(jnp.float32),
    )
    middle_num = numerator[rim:-rim]
    middle_den = denominator[rim:-rim]
    middle_num = middle_num.at[:rim].add(from_prev[0]).at[-rim:].add(from_next[0])
    middle_den = middle_den.at[:rim].add(from_prev[1]).at[-rim:].add(from_next[1])
    return (middle_num, middle_den)


def fold_cols(numerator, denominator, rim):
    from_next = (
        shifted(numerator[:, :rim].astype(jnp.bfloat16), "col", -1).astype(jnp.float32),
        shifted(denominator[:, :rim].astype(jnp.bfloat16), "col", -1).astype(jnp.float32),
    )
    from_prev = (
        shifted(numerator[:, -rim:].astype(jnp.bfloat16), "col", 1).astype(jnp.float32),
        shifted(denominator[:, -rim:].astype(jnp.bfloat16), "col", 1).astype(jnp.float32),
    )
    middle_num = numerator[:, rim:-rim] + jnp.concatenate([from_prev[0], from_next[0]], axis=1)
    middle_den = denominator[:, rim:-rim] + jnp.concatenate([from_prev[1], from_next[1]], axis=1)
    return (middle_num, middle_den)


def body(embeddings, pos_embed, ln_gain, ln_bias, w_qkv, b_qkv, w_out, b_out, valid):
    tile = embeddings.shape[1]
    tile_rows = embeddings.shape[0] // tile
    rim = tile // 2
    win = tile + 2 * rim
    rows_count = win * win
    width_model = embeddings.shape[2]
    window = extended(embeddings, (("row", 0), ("col", 1)), rim)
    stacked = jnp.stack([window], axis=0)
    inputs = stacked.reshape(tile_rows, rows_count, width_model).astype(
        jnp.float32
    ) + pos_embed.astype(jnp.float32)
    inputs = inputs.reshape(tile_rows * rows_count, width_model)
    normed = layer_norm(inputs, ln_gain, ln_bias).astype(jnp.bfloat16)
    projected = jnp.dot(
        normed,
        lax.all_gather(w_qkv, ("row", "col"), axis=0, tiled=True),
        preferred_element_type=jnp.float32,
    )
    projected = (
        (projected + b_qkv).astype(jnp.bfloat16).reshape(tile_rows, rows_count, w_qkv.shape[1])
    )
    attended = jax.vmap(attend)(projected).reshape(tile_rows * rows_count, -1)
    projected_out = lax.dot_general(
        attended,
        lax.all_gather(w_out, ("row", "col"), axis=0, tiled=True),
        (((1,), (1,)), ((), ())),
        preferred_element_type=jnp.float32,
    )
    hidden = inputs + projected_out + b_out
    gauss = gauss_table(win).reshape(1, rows_count)
    weight = gauss * valid.reshape(tile_rows, rows_count).astype(jnp.float32) / 196.0
    contrib = (weight.reshape(tile_rows * rows_count, 1) * hidden).reshape(
        tile_rows, win, win, width_model
    )
    weight_grid = weight.reshape(tile_rows, win, win)
    numerator = jnp.zeros((tile_rows * tile + 2 * rim, win, width_model), jnp.float32)
    denominator = jnp.zeros((tile_rows * tile + 2 * rim, win), jnp.float32)
    numerator = numerator.at[0:win].add(contrib[0])
    denominator = denominator.at[0:win].add(weight_grid[0])
    numerator, denominator = fold_rows(numerator, denominator, rim)
    numerator, denominator = fold_cols(numerator, denominator, rim)
    return (numerator / jnp.maximum(denominator, FLOOR)[:, :, None]).astype(jnp.bfloat16)


def solution(mesh):
    placed = (
        P(("groups", "row"), "col", None),
        P(),
        P(),
        P(),
        P(("row", "col"), None),
        P(),
        P(("row", "col"), None),
        P(),
        P(("groups", "row"), "col", None),
    )
    rows = mesh.shape["row"]

    def run(*arrays):
        embeddings, w_qkv = arrays[0], arrays[4]
        tile = embeddings.shape[1]
        whole_tiles = w_qkv.shape[0] % 16 == 0 and embeddings.shape[0] == tile == 8
        pairs = mesh.shape["groups"] == 2 and mesh.shape["col"] == 2
        if whole_tiles and pairs and rows == 8:
            return fused(rows, *arrays)
        return body(*arrays)

    return jax.shard_map(
        run,
        mesh=mesh,
        in_specs=placed,
        out_specs=P(("groups", "row"), "col", None),
        check_vma=False,
    )
```
